512 devices in a mesh: az: 32 (over z, x_lo), rad: 16 (over y, x_hi, core).
Axes of the slice: x: 4 (x_hi: 2, x_lo: 2; x = x_hi * 2 + x_lo), y: 4, z: 16, core: 2. Of those that a mesh axis runs over, the one named last changes fastest.
Arguments:
- potential: float32 [3, 3, 8192, 2048], P(None, None, 'az', 'rad'), may hold values from -6 to 6
- current: float32 [3, 3, 8192, 2048], P(None, None, 'az', 'rad'), may hold values from -24 to 24
- material: int32 [3, 8192, 2048], P(None, 'az', 'rad'), may hold values from 0 to 7
- nu_table: float32 [8], replicated, may hold values from 0.2 to 2
- sat_table: float32 [8], replicated, may hold values from 0.2 to 3
- panel_flux: float32 [9, 8192], P(None, 'az'), may hold values from -48 to 48
- panel_jitter: int32 [8192], P('az'), may hold values from 0 to 8191
- rotor_offset: int32 [1], replicated, may hold values from 0 to 8191
Outputs:
- updated: float32 [3, 3, 8192, 2048], P(None, None, 'az', 'rad')
The draws below stay inside these ranges and needn't reach their ends.
All inputs are finite; a program needn't handle non-finite values.
Results may differ from the reference program's by a relative error of at most 0.000064.
Values sent between devices are 32-bit elements; how exact they have to be, the bound alone decides.
A program may use at most 64 MiB of HBM per device.

```python
import math
import jax
import jax.numpy as jnp

L = 3
MAT = 8
NA = 8192
NR = 2048
NPAN = 8192


def with_ends(array, key, low, largest):
    longest = array.shape.index(max(array.shape))
    spots = []
    for shift in (0, 1):
        where = [jax.random.randint(jax.random.fold_in(key, axis), (), 0, length) for axis, length in enumerate(array.shape)]
        where[longest] = (where[longest] + shift) % array.shape[longest]
        spots.append(tuple(where))
    return array.at[spots[0]].set(low).at[spots[1]].set(largest)


def level_of(key, shape, pieces, low, largest):
    def one(dim, parts):
        heights = jax.random.uniform(jax.random.fold_in(jax.random.fold_in(key, 6), dim), (parts,), jnp.float32, low / len(pieces), largest / len(pieces))
        return jnp.repeat(jnp.exp(heights), shape[dim] // parts).reshape((-1,) + (1,) * (len(shape) - dim - 1))

    loudness = one(*pieces[0])
    for cut in pieces[1:]:
        loudness = loudness * one(*cut)
    return loudness


def bell_draw(rng, dims, scale, bound, split=(), kind=jnp.bfloat16):
    level = level_of(rng, dims, split, -0.22, 0.18) if split else 1.0
    drawn = jax.random.normal(rng, dims, jnp.float32) * scale * level
    return jnp.minimum(jnp.maximum(drawn, -bound), bound).astype(kind)


def setup_inputs(seed: int = 0) -> dict:
    key_list = jax.random.split(jax.random.key(seed), 9)
    potential = bell_draw(key_list[0], (3, L, NA, NR), 1.0, 6.0, ((2, 32), (3, 16)), jnp.float32)
    current = bell_draw(key_list[1], (3, L, NA, NR), 4.0, 24.0, ((2, 32), (3, 16)), jnp.float32)
    material = with_ends(jax.random.randint(key_list[2], (L, NA, NR), 0, MAT), jax.random.fold_in(key_list[2], 1), 0, MAT - 1).astype(jnp.int32)
    nu_table = jnp.clip(jnp.exp(jax.random.uniform(key_list[3], (MAT,), jnp.float32, math.log(0.2), math.log(2.0))), 0.2, 2.0)
    sat_table = jnp.clip(jnp.exp(jax.random.uniform(key_list[4], (MAT,), jnp.float32, math.log(0.2), math.log(3.0))), 0.2, 3.0)
    panel_flux = bell_draw(key_list[5], (3 * L, NPAN), 8.0, 48.0, ((1, 32),), jnp.float32)
    panel_jitter = with_ends(jax.random.randint(key_list[6], (NPAN,), 0, NA), jax.random.fold_in(key_list[6], 1), 0, NA - 1).astype(jnp.int32)
    rotor_offset = jax.random.randint(key_list[7], (1,), 0, NA).astype(jnp.int32)
    return dict(potential=potential, current=current, material=material, nu_table=nu_table, sat_table=sat_table, panel_flux=panel_flux, panel_jitter=panel_jitter, rotor_offset=rotor_offset)


sigma_term = 1.0
neighbour_steps = ((0, 1, 0), (0, -1, 0), (0, 0, 1), (0, 0, -1), (1, 0, 0), (-1, 0, 0))


def lookup(material, values_table):
    result = jnp.zeros(material.shape, values_table.dtype)
    for entry in range(values_table.shape[0]):
        result = result + jnp.where(material == entry, values_table[entry], jnp.zeros((), values_table.dtype))
    return result


def extend_cells(field):
    wrapped = jnp.concatenate([field[:, :, -1:], field, field[:, :, :1]], axis=2)
    return jnp.pad(wrapped, ((0, 0), (0, 0), (0, 0), (1, 1)))


def strength(extended):
    centre = extended[:, :, 1:-1, 1:-1]
    azimuth_diff = extended[:, :, 2:, 1:-1] - centre
    radial_diff = extended[:, :, 1:-1, 2:] - centre
    return jnp.sum(azimuth_diff * azimuth_diff + radial_diff * radial_diff, axis=0, keepdims=True)


def offset_view(field, layer_step, az_step, rad_step):
    return field[:, 1 + layer_step:field.shape[1] - 1 + layer_step, 1 + az_step:field.shape[2] - 1 + az_step, 1 + rad_step:field.shape[3] - 1 + rad_step]


def jacobi_sweep(field, coef, source):
    padded_field = jnp.pad(field, ((0, 0), (1, 1), (0, 0), (0, 0)))
    padded_coef = jnp.pad(coef, ((0, 0), (1, 1), (0, 0), (0, 0)))
    centre = offset_view(padded_coef, 0, 0, 0)
    numerator = source
    denominator = jnp.full_like(centre, sigma_term)
    for layer_step, az_step, rad_step in neighbour_steps:
        face_coef = 0.5 * (centre + offset_view(padded_coef, layer_step, az_step, rad_step))
        numerator = numerator + face_coef * offset_view(padded_field, layer_step, az_step, rad_step)
        denominator = denominator + face_coef
    return numerator / denominator


def reference(potential, current, material, nu_table, sat_table, panel_flux, panel_jitter, rotor_offset):
    position = (rotor_offset[0] + panel_jitter) % NA
    airgap = jax.ops.segment_sum(panel_flux.T, position, num_segments=NA).T.reshape(3, L, NA)
    source = current.at[:, :, :, NR // 2].add(airgap)
    base_reluct = lookup(material, nu_table)[None]
    saturation = lookup(material, sat_table)[None]
    extended = extend_cells(potential)
    flux_sq = strength(extended)
    reluct = base_reluct * (1.0 + saturation * flux_sq / (1.0 + flux_sq))
    reluct_wide = extend_cells(reluct)
    sweep_one = jacobi_sweep(extended, reluct_wide, source)
    return jacobi_sweep(extend_cells(sweep_one), reluct_wide, source)
```

```python
import jax
import jax.numpy as jnp
from jax import lax
from jax.experimental import pallas as pl
from jax.experimental.pallas import tpu as pltpu
from jax.sharding import PartitionSpec as P

MESH = pl.DeviceIdType.MESH
F32 = jnp.float32
L, NF, MAT = 3, 9, 8
B = 16
LANES = 128
STRIP = 384
TO_LEFT, TO_RIGHT = 48, 40


def lookup(material, table):
    low, mid, high = [(material & bit) != 0 for bit in (1, 2, 4)]
    pairs = [jnp.where(low, table[2 * i + 1], table[2 * i]) for i in range(4)]
    quads = [jnp.where(mid, pairs[2 * i + 1], pairs[2 * i]) for i in range(2)]
    return jnp.where(high, quads[1], quads[0])


def half_reluct(material, flux_sq, nu_half, sat):
    return lookup(material, nu_half) * (1.0 + lookup(material, sat) * flux_sq / (1.0 + flux_sq))


def sweep(values, source, faces, inverse):
    total = source
    for face, value in zip(faces, values):
        if value is not None:
            total = total + face * value
    return total * inverse


def kernel(
    pot, cur, mat, nu, sat, flux, jitter, offset, out,
    a_ext, c_ext, m_ext, q_ext, inv_ext, v_ext,
    to_prev, to_next, from_prev, from_next,
    left_main, left_corner, right_main, right_corner,
    in_right_main, in_right_corner, in_left_main, in_left_corner,
    s_a, s_m, s_c, s_q, s_inv, s_v,
    block, land, acc, spread,
    load_sem, az_send, az_recv, rad_send, rad_recv, pan_send, pan_recv,
):
    az, rad = lax.axis_index("az"), lax.axis_index("rad")
    n_az, n_rad = lax.axis_size("az"), lax.axis_size("rad")
    n_z = n_az // 2
    rows = pot.shape[1]
    cells = rows * n_az
    z, x = az // 2, az % 2
    stator = n_rad // 2
    gap = (rad == stator) | (rad == stator - 1)
    has_left, has_right = rad > 0, rad < n_rad - 1
    reach_z = z + n_z // 2
    slot_k = reach_z % n_z
    direct = gap & (az != 0) & (slot_k >= 0) & ((slot_k < 6) | (slot_k > 10))

    def place(dz, dx):
        return (((z + dz + n_z) % n_z) * 2 + (x + dx) % 2, rad)

    loads = [
        pltpu.make_async_copy(pot, a_ext.at[:, pl.ds(B, rows), :], load_sem.at[0]),
        pltpu.make_async_copy(cur, c_ext.at[:, pl.ds(B, rows), :], load_sem.at[1]),
        pltpu.make_async_copy(mat, m_ext.at[:, pl.ds(B, rows), :], load_sem.at[2]),
    ]
    for load in loads:
        load.start()

    bar = pltpu.get_barrier_semaphore()
    prev, nxt = (az + n_az - 1) % n_az, (az + 1) % n_az

    def greet(who):
        pl.semaphore_signal(bar, inc=1, device_id=who, device_id_type=MESH)

    greet((prev, rad))
    greet((nxt, rad))

    @pl.when(has_left)
    def _():
        greet((az, rad - 1))

    @pl.when(has_right)
    def _():
        greet((az, rad + 1))

    window = [(dz, dx) for dz in (-2, -1, 0, 1, 2) for dx in (0, 1) if (dz, dx) != (0, 0)]

    @pl.when(gap)
    def _():
        for dz, dx in window:
            greet(place(dz, dx))

        @pl.when(az != 0)
        def _():
            greet(place(-3, 0))
            greet(place(3, 0))

        @pl.when(az == 0)
        def _():
            for far in range(3, n_z - 2):
                for side in (0, 1):
                    greet((far * 2 + side, rad))

    up_ok = jnp.logical_not((z == n_z - 3) & (x == 0))
    down_ok = jnp.logical_not((z == 3) & (x == 0))
    one = lambda flag: jnp.where(flag, 1, 0).astype(jnp.int32)
    expected = 2 + one(has_left) + one(has_right)
    expected = expected + one(gap) * (len(window) + one(up_ok) + one(down_ok)) + one(direct)

    half = rows // 2
    block[0:8, :] = flux[0:8, 0:half]
    block[8:16, :] = flux[0:8, half:rows]
    block[16:17, :] = flux[8:9, 0:half]
    block[17:18, :] = flux[8:9, half:rows]
    for part in (0, 1):
        turned = offset[0] + jitter[pl.ds(part * half, half)].reshape(1, half)
        turned = jnp.where(turned >= cells, turned - cells, turned)
        block[18 + part : 19 + part, :] = turned.astype(F32)
    block[20:24, :] = jnp.zeros((4, half), F32)

    for buf, count in ((a_ext, NF), (c_ext, NF), (m_ext, L)):
        for i in range(count):
            buf[i, 0:B, :] = jnp.zeros((B, LANES), buf.dtype)
            buf[i, B + rows : B + rows + B, :] = jnp.zeros((B, LANES), buf.dtype)

    pl.semaphore_wait(bar, expected)

    def panels(src, dst, send, recv, who):
        return pltpu.make_async_remote_copy(
            src_ref=src, dst_ref=dst, send_sem=pan_send.at[send], recv_sem=pan_recv.at[recv],
            device_id=who, device_id_type=MESH)

    def direct_copy(recv):
        return panels(block, land.at[slot_k * 2 + x], 9, recv, (0, rad))

    window_copies = [
        panels(block, land.at[(8 - dz) * 2 + x], i, 0, place(dz, dx)) for i, (dz, dx) in enumerate(window)
    ]
    own_copy = pltpu.make_async_copy(block, land.at[16 + x], pan_recv.at[0])
    far_regions = ((1, 3, 6), (2, 11, 14), (3, 0, 3), (4, 14, 16))

    @pl.when(gap)
    def _():
        for recv, low, high in far_regions:

            @pl.when(direct & (slot_k >= low) & (slot_k < high))
            def _():
                direct_copy(recv).start()

        for copy in window_copies:
            copy.start()
        own_copy.start()

    for load in loads:
        load.wait()
    last = B + rows
    for f in range(NF):
        to_prev[3 * f : 3 * f + 3, :] = a_ext[f, B : B + 3, :]
        to_prev[33 + f : 34 + f, :] = c_ext[f, B : B + 1, :]
        to_next[2 * f : 2 * f + 2, :] = a_ext[f, last - 2 : last, :]
        to_next[24 + f : 25 + f, :] = c_ext[f, last - 1 : last, :]
    for l in range(L):
        to_prev[27 + 2 * l : 29 + 2 * l, :] = m_ext[l, B : B + 2, :].astype(F32)
        to_next[18 + 2 * l : 20 + 2 * l, :] = m_ext[l, last - 2 : last, :].astype(F32)
    to_prev[42:48, :] = jnp.zeros((6, LANES), F32)
    to_next[33:40, :] = jnp.zeros((7, LANES), F32)

    def az_copy(src, dst, i, who):
        return pltpu.make_async_remote_copy(
            src_ref=src, dst_ref=dst, send_sem=az_send.at[i], recv_sem=az_recv.at[i],
            device_id=(who, rad), device_id_type=MESH)

    down_copy = az_copy(to_prev, from_next, 0, prev)
    up_copy = az_copy(to_next, from_prev, 1, nxt)
    down_copy.start()
    up_copy.start()

    def to_strip(f, dst, tile, lanes):
        turned = tile.T
        dst[f, 2:8, lanes] = turned[0:6]
        dst[f, 8:13, lanes] = turned[LANES - 5 : LANES]

    def pack(count, lanes, left, right):
        for f in range(NF):
            left[3 * f : 3 * f + 3, :] = s_a[f, 2:5, lanes]
            left[33 + f : 34 + f, :] = s_c[f, 2:3, lanes]
            right[2 * f : 2 * f + 2, :] = s_a[f, 11:13, lanes]
            right[24 + f : 25 + f, :] = s_c[f, 12:13, lanes]
        for l in range(L):
            left[27 + 2 * l : 29 + 2 * l, :] = s_m[l, 2:4, lanes]
            right[18 + 2 * l : 20 + 2 * l, :] = s_m[l, 11:13, lanes]
        left[42:48, :] = jnp.zeros((6, count), F32)
        right[33:40, :] = jnp.zeros((7, count), F32)

    def rad_copy(src, dst, i, who):
        return pltpu.make_async_remote_copy(
            src_ref=src, dst_ref=dst, send_sem=rad_send.at[i], recv_sem=rad_recv.at[i],
            device_id=(az, who), device_id_type=MESH)

    left_copies = (rad_copy(left_main, in_right_main, 0, rad - 1), rad_copy(left_corner, in_right_corner, 1, rad - 1))
    right_copies = (rad_copy(right_main, in_left_main, 2, rad + 1), rad_copy(right_corner, in_left_corner, 3, rad + 1))

    def send_strips(i):
        @pl.when(has_left)
        def _():
            left_copies[i].start()

        @pl.when(has_right)
        def _():
            right_copies[i].start()

    @pl.loop(0, NF)
    def _(f):
        for part in (0, 1):
            lanes = slice(part * LANES, (part + 1) * LANES)
            to_strip(f, s_a, a_ext[f, B + part * LANES : B + (part + 1) * LANES, :], lanes)
            to_strip(f, s_c, c_ext[f, B + part * LANES : B + (part + 1) * LANES, :], lanes)

    @pl.loop(0, L)
    def _(l):
        for part in (0, 1):
            lanes = slice(part * LANES, (part + 1) * LANES)
            to_strip(l, s_m, m_ext[l, B + part * LANES : B + (part + 1) * LANES, :].astype(F32), lanes)

    pack(rows, slice(0, rows), left_main, right_main)
    send_strips(0)

    down_copy.wait()
    up_copy.wait()
    for f in range(NF):
        a_ext[f, last : last + 3, :] = from_next[3 * f : 3 * f + 3, :]
        c_ext[f, last : last + 1, :] = from_next[33 + f : 34 + f, :]
        a_ext[f, B - 2 : B, :] = from_prev[2 * f : 2 * f + 2, :]
        c_ext[f, B - 1 : B, :] = from_prev[24 + f : 25 + f, :]
    for l in range(L):
        m_ext[l, last : last + 2, :] = from_next[27 + 2 * l : 29 + 2 * l, :].astype(jnp.int32)
        m_ext[l, B - 2 : B, :] = from_prev[18 + 2 * l : 20 + 2 * l, :].astype(jnp.int32)

    def rim(buf, f):
        gap_rows = jnp.zeros((LANES - 16, LANES), F32)
        return jnp.concatenate(
            [buf[f, last : last + 8, :].astype(F32), gap_rows, buf[f, B - 8 : B, :].astype(F32)], axis=0
        )

    ends = slice(rows, STRIP)

    @pl.loop(0, NF)
    def _(f):
        to_strip(f, s_a, rim(a_ext, f), ends)
        to_strip(f, s_c, rim(c_ext, f), ends)

    @pl.loop(0, L)
    def _(l):
        to_strip(l, s_m, rim(m_ext, l), ends)

    pack(LANES, ends, left_corner, right_corner)
    send_strips(1)

    nu_half = [nu[i] * 0.5 for i in range(MAT)]
    sat_of = [sat[i] for i in range(MAT)]

    @pl.loop(0, rows // 8 + 2)
    def _(i):
        e = pl.multiple_of(i * 8 + 8, 8)
        for l in range(L):
            flux_sq = jnp.zeros((8, LANES), F32)
            for c in range(3):
                here = a_ext[c * L + l, pl.ds(e, 8), :]
                along = a_ext[c * L + l, pl.ds(e + 1, 8), :] - here
                across = pltpu.roll(here, LANES - 1, 1) - here
                flux_sq = flux_sq + along * along + across * across
            q_ext[l, pl.ds(e, 8), :] = half_reluct(m_ext[l, pl.ds(e, 8), :], flux_sq, nu_half, sat_of)

    def region(low, high, recv):
        view = land.at[pl.ds(low, high - low)]
        return pltpu.make_async_copy(view, view, pan_recv.at[recv])

    two_up = panels(land.at[pl.ds(12, 6)], land.at[pl.ds(6, 6)], 10, 1, place(3, 0))
    two_down = panels(land.at[pl.ds(16, 6)], land.at[pl.ds(22, 6)], 11, 2, place(-3, 0))
    three_up = panels(land.at[pl.ds(6, 6)], land.at[pl.ds(0, 6)], 12, 3, place(3, 0))
    three_down = panels(land.at[pl.ds(22, 4)], land.at[pl.ds(28, 4)], 13, 4, place(-3, 0))

    def when_start(flag, copy):
        @pl.when(flag)
        def _():
            copy.start()

    @pl.when(gap)
    def _():
        region(12, 22, 0).wait()
        when_start(up_ok, two_up)
        when_start(down_ok, two_down)

    def faces_of(q, q_next, q_prev, q_right, q_left, q_above, q_below):
        faces = [q + q_next, q + q_prev, q + q_right, q + q_left]
        faces.append(q if q_above is None else q + q_above)
        faces.append(q if q_below is None else q + q_below)
        return faces

    def main_faces(e, l):
        q = q_ext[l, pl.ds(e, 8), :]
        return faces_of(
            q, q_ext[l, pl.ds(e + 1, 8), :], q_ext[l, pl.ds(e - 1, 8), :],
            pltpu.roll(q, LANES - 1, 1), pltpu.roll(q, 1, 1),
            q_ext[l + 1, pl.ds(e, 8), :] if l + 1 < L else None, q_ext[l - 1, pl.ds(e, 8), :] if l > 0 else None)

    def main_neighbours(field, e, c, l):
        here = field[c * L + l, pl.ds(e, 8), :]
        return [
            field[c * L + l, pl.ds(e + 1, 8), :], field[c * L + l, pl.ds(e - 1, 8), :],
            pltpu.roll(here, LANES - 1, 1), pltpu.roll(here, 1, 1),
            field[c * L + l + 1, pl.ds(e, 8), :] if l + 1 < L else None,
            field[c * L + l - 1, pl.ds(e, 8), :] if l > 0 else None]

    @pl.loop(0, rows // 8 + 2)
    def _(i):
        e = pl.multiple_of(i * 8 + 8, 8)
        for l in range(L):
            faces = main_faces(e, l)
            inverse = 1.0 / (1.0 + sum(faces[1:], faces[0]))
            inv_ext[l, pl.ds(e, 8), :] = inverse
            for c in range(3):
                source = c_ext[c * L + l, pl.ds(e, 8), :]
                v_ext[c * L + l, pl.ds(e, 8), :] = sweep(main_neighbours(a_ext, e, c, l), source, faces, inverse)

    @pl.when(gap)
    def _():
        region(6, 12, 1).wait()
        region(22, 28, 2).wait()
        when_start(up_ok, three_up)
        when_start(down_ok, three_down)

    @pl.loop(0, rows // 8)
    def _(i):
        e = pl.multiple_of(i * 8 + B, 8)
        for l in range(L):
            faces = main_faces(e, l)
            inverse = inv_ext[l, pl.ds(e, 8), :]
            for c in range(3):
                source = c_ext[c * L + l, pl.ds(e, 8), :]
                out[c * L + l, pl.ds(e - B, 8), :] = sweep(main_neighbours(v_ext, e, c, l), source, faces, inverse)

    for f in range(NF):
        s_c[f, 0:2, :] = jnp.zeros((2, STRIP), F32)
        s_c[f, 13:16, :] = jnp.zeros((3, STRIP), F32)
    for l in range(L):
        s_m[l, 15:16, :] = jnp.zeros((1, STRIP), F32)

    @pl.when(has_right)
    def _():
        for i, (came, lanes) in enumerate(((in_right_main, slice(0, rows)), (in_right_corner, ends))):
            rad_copy(left_main if i == 0 else left_corner, came, i, rad + 1).wait_recv()
            for f in range(NF):
                s_a[f, 13:16, lanes] = came[3 * f : 3 * f + 3, :]
                s_c[f, 13:14, lanes] = came[33 + f : 34 + f, :]
            for l in range(L):
                s_m[l, 13:15, lanes] = came[27 + 2 * l : 29 + 2 * l, :]

    @pl.when(has_left)
    def _():
        for i, (came, lanes) in enumerate(((in_left_main, slice(0, rows)), (in_left_corner, ends))):
            rad_copy(right_main if i == 0 else right_corner, came, i + 2, rad - 1).wait_recv()
            for f in range(NF):
                s_a[f, 0:2, lanes] = came[2 * f : 2 * f + 2, :]
                s_c[f, 1:2, lanes] = came[24 + f : 25 + f, :]
            for l in range(L):
                s_m[l, 0:2, lanes] = came[18 + 2 * l : 20 + 2 * l, :]

    @pl.when(jnp.logical_not(has_right))
    def _():
        for f in range(NF):
            s_a[f, 13:16, :] = jnp.zeros((3, STRIP), F32)
        for l in range(L):
            s_m[l, 13:15, :] = jnp.zeros((2, STRIP), F32)

    @pl.when(jnp.logical_not(has_left))
    def _():
        for f in range(NF):
            s_a[f, 0:2, :] = jnp.zeros((2, STRIP), F32)
        for l in range(L):
            s_m[l, 0:2, :] = jnp.zeros((2, STRIP), F32)

    column = lax.broadcasted_iota(jnp.int32, (16, STRIP), 0)
    outside = ((column < 2) & (rad == 0)) | ((column > 12) & (rad == n_rad - 1))
    after = lambda v: pltpu.roll(v, STRIP - 1, 1)
    before = lambda v: pltpu.roll(v, 1, 1)
    right_of = lambda v: pltpu.roll(v, 15, 0)
    left_of = lambda v: pltpu.roll(v, 1, 0)

    for l in range(L):
        flux_sq = jnp.zeros((16, STRIP), F32)
        for c in range(3):
            here = s_a[c * L + l]
            along, across = after(here) - here, right_of(here) - here
            flux_sq = flux_sq + along * along + across * across
        q = half_reluct(s_m[l].astype(jnp.int32), flux_sq, nu_half, sat_of)
        s_q[l] = jnp.where(outside, 0.0, q)

    def strip_faces(l):
        q = s_q[l]
        return faces_of(
            q, after(q), before(q), right_of(q), left_of(q),
            s_q[l + 1] if l + 1 < L else None, s_q[l - 1] if l > 0 else None)

    def strip_neighbours(field, c, l):
        here = field[c * L + l]
        return [
            after(here), before(here), right_of(here), left_of(here),
            field[c * L + l + 1] if l + 1 < L else None, field[c * L + l - 1] if l > 0 else None]

    for l in range(L):
        faces = strip_faces(l)
        inverse = 1.0 / (1.0 + sum(faces[1:], faces[0]))
        s_inv[l] = inverse
        for c in range(3):
            swept = sweep(strip_neighbours(s_a, c, l), s_c[c * L + l], faces, inverse)
            s_v[c * L + l] = jnp.where(outside, 0.0, swept)

    def deposit(low, high):
        @pl.loop(low, high)
        def _(slot):
            parts = []
            for part in (0, 1):
                cell = land[slot, 18 + part : 19 + part, :].astype(jnp.int32) - az * rows
                cell = jnp.where(cell < 0, cell + cells, cell)
                ahead = jnp.where(cell < rows + 8, cell, -1)
                cell = jnp.where(cell >= cells - 8, cell - (cells - 8) + rows + 8, ahead)
                places = lax.broadcasted_iota(jnp.int32, (rows + 16, half), 0)
                parts.append(jnp.where(places == cell, 1.0, 0.0).astype(jnp.bfloat16))
            onehot = jnp.concatenate(parts, axis=1)
            top = jnp.concatenate([land[slot, 0:8, :], land[slot, 8:16, :]], axis=1)
            ninth = jnp.concatenate([land[slot, 16:17, :], land[slot, 17:18, :]], axis=1)
            values = jnp.concatenate([top, ninth, jnp.zeros((7, rows), F32)], axis=0)
            first = values.astype(jnp.bfloat16)
            rest = values - first.astype(F32)
            second = rest.astype(jnp.bfloat16)
            third = (rest - second.astype(F32)).astype(jnp.bfloat16)
            terms = jnp.concatenate([first, second, third], axis=0)
            acc[...] += lax.dot_general(
                onehot, terms, (((1,), (1,)), ((), ())), preferred_element_type=F32
            )

    @pl.when(gap)
    def _():
        acc[...] = jnp.zeros_like(acc)
        spread[...] = jnp.zeros_like(spread)
        deposit(6, 28)
        region(0, 6, 3).wait()
        region(28, 32, 4).wait()
        deposit(0, 6)
        deposit(28, 32)
        spread[0 : rows + 8, 0:48] = acc[0 : rows + 8, :]
        spread[STRIP - 8 : STRIP, 0:48] = acc[rows + 8 : rows + 16, :]
        turned = jnp.concatenate(
            [spread[i * LANES : (i + 1) * LANES, :].T for i in range(3)], axis=1
        )
        airgap = turned[0:16] + turned[16:32] + turned[32:48]

        @pl.when(rad == stator)
        def _():
            for f in range(NF):
                row = airgap[f : f + 1]
                s_c[f, 2:3, :] = s_c[f, 2:3, :] + row
                s_v[f, 2:3, :] = s_v[f, 2:3, :] + row * s_inv[f % L, 2:3, :]

        @pl.when(rad == stator - 1)
        def _():
            for f in range(NF):
                s_v[f, 13:14, :] = s_v[f, 13:14, :] + airgap[f : f + 1] * s_inv[f % L, 13:14, :]

    lane = lax.broadcasted_iota(jnp.int32, (LANES, LANES), 1)
    edge = (lane < 2) | (lane > LANES - 4)
    for l in range(L):
        faces = strip_faces(l)
        for c in range(3):
            f = c * L + l
            done = sweep(strip_neighbours(s_v, c, l), s_c[f], faces, s_inv[l])
            for part in (0, 1):
                piece = done[:, part * LANES : (part + 1) * LANES]
                tall = jnp.concatenate([piece[2:10], jnp.zeros((LANES - 16, LANES), F32), piece[5:13]], axis=0)
                own = out[f, part * LANES : (part + 1) * LANES, :]
                out[f, part * LANES : (part + 1) * LANES, :] = jnp.where(edge, tall.T, own)

    for i in (0, 1):
        @pl.when(has_left)
        def _():
            left_copies[i].wait_send()

        @pl.when(has_right)
        def _():
            right_copies[i].wait_send()

    @pl.when(gap)
    def _():
        for copy in window_copies:
            copy.wait_send()

        @pl.when(direct)
        def _():
            direct_copy(1).wait_send()

        @pl.when(up_ok)
        def _():
            two_up.wait_send()
            three_up.wait_send()

        @pl.when(down_ok)
        def _():
            two_down.wait_send()
            three_down.wait_send()


def local(potential, current, material, nu_table, sat_table, panel_flux, panel_jitter, rotor_offset):
    rows, lanes = potential.shape[2:]
    vmem = lambda *shape: pltpu.VMEM(shape, F32)
    tall = rows + 2 * B
    any_spec = pl.BlockSpec(memory_space=pl.ANY)
    smem = pl.BlockSpec(memory_space=pltpu.SMEM)
    whole = pl.BlockSpec(memory_space=pltpu.VMEM)
    result = pl.pallas_call(
        kernel,
        out_shape=jax.ShapeDtypeStruct((NF, rows, lanes), F32),
        in_specs=[any_spec, any_spec, any_spec, smem, smem, whole, whole, smem],
        out_specs=whole,
        scratch_shapes=[
            vmem(NF, tall, lanes), vmem(NF, tall, lanes), pltpu.VMEM((L, tall, lanes), jnp.int32),
            vmem(L, tall, lanes), vmem(L, tall, lanes), vmem(NF, tall, lanes),
            vmem(TO_LEFT, lanes), vmem(TO_RIGHT, lanes), vmem(TO_RIGHT, lanes), vmem(TO_LEFT, lanes),
            vmem(TO_LEFT, rows), vmem(TO_LEFT, LANES), vmem(TO_RIGHT, rows), vmem(TO_RIGHT, LANES),
            vmem(TO_LEFT, rows), vmem(TO_LEFT, LANES), vmem(TO_RIGHT, rows), vmem(TO_RIGHT, LANES),
            vmem(NF, 16, STRIP), vmem(L, 16, STRIP), vmem(NF, 16, STRIP),
            vmem(L, 16, STRIP), vmem(L, 16, STRIP), vmem(NF, 16, STRIP),
            vmem(24, LANES), vmem(32, 24, LANES), vmem(rows + 16, 48), vmem(STRIP, LANES),
            pltpu.SemaphoreType.DMA((3,)), pltpu.SemaphoreType.DMA((2,)), pltpu.SemaphoreType.DMA((2,)),
            pltpu.SemaphoreType.DMA((4,)), pltpu.SemaphoreType.DMA((4,)),
            pltpu.SemaphoreType.DMA((14,)), pltpu.SemaphoreType.DMA((5,)),
        ],
        compiler_params=pltpu.CompilerParams(
            collective_id=0, has_side_effects=True, vmem_limit_bytes=48 * 1024 * 1024
        ),
    )(
        potential.reshape(NF, rows, lanes), current.reshape(NF, rows, lanes), material,
        nu_table, sat_table, panel_flux, panel_jitter, rotor_offset,
    )
    return result.reshape(potential.shape)


def solution(mesh):
    placed = (
        P(None, None, "az", "rad"),
        P(None, None, "az", "rad"),
        P(None, "az", "rad"),
        P(),
        P(),
        P(None, "az"),
        P("az"),
        P(),
    )
    return jax.shard_map(
        local, mesh=mesh, in_specs=placed, out_specs=P(None, None, "az", "rad"), check_vma=False
    )
```

```python
import jax
import jax.numpy as jnp
from jax import lax
from jax.experimental import pallas as pl
from jax.experimental.pallas import tpu as pltpu
from jax.sharding import PartitionSpec as P

MESH = pl.DeviceIdType.MESH
F32 = jnp.float32
L, NF, MAT = 3, 9, 8
B = 16
LANES = 128
STRIP = 384
TO_LEFT, TO_RIGHT = 48, 40


def lookup(material, table):
    low, mid, high = [(material & bit) != 0 for bit in (1, 2, 4)]
    pairs = [jnp.where(low, table[2 * i + 1], table[2 * i]) for i in range(4)]
    quads = [jnp.where(mid, pairs[2 * i + 1], pairs[2 * i]) for i in range(2)]
    return jnp.where(high, quads[1], quads[0])


def half_reluct(material, flux_sq, nu_half, sat):
    return lookup(material, nu_half) * (1.0 + lookup(material, sat) * flux_sq / (1.0 + flux_sq))


def sweep(values, source, faces, inverse):
    total = source
    for face, value in zip(faces, values):
        if value is not None:
            total = total + face * value
    return total * inverse


def kernel(
    pot, cur, mat, nu_hbm, sat_hbm, flux_hbm, jitter_hbm, offset, out,
    nu, sat, flux, jitter,
    a_ext, c_ext, m_ext, q_ext, inv_ext, v_ext,
    to_prev, to_next, from_prev, from_next,
    left_main, left_corner, right_main, right_corner,
    in_right_main, in_right_corner, in_left_main, in_left_corner,
    s_a, s_m, s_c, s_q, s_inv, s_v,
    block, land, acc, spread, stacked,
    load_sem, az_send, az_recv, rad_send, rad_recv, pan_send, pan_recv,
):
    az, rad = lax.axis_index("az"), lax.axis_index("rad")
    n_az, n_rad = lax.axis_size("az"), lax.axis_size("rad")
    n_z = n_az // 2
    rows = pot.shape[1]
    cells = rows * n_az
    z, x = az // 2, az % 2
    stator = n_rad // 2
    gap = (rad == stator) | (rad == stator - 1)
    has_left, has_right = rad > 0, rad < n_rad - 1
    reach_z = z + n_z // 2
    slot_k = reach_z % n_z
    direct = gap & (az != 0) & (slot_k >= 0) & ((slot_k < 6) | (slot_k > 10))

    def place(dz, dx):
        return (((z + dz + n_z) % n_z) * 2 + (x + dx) % 2, rad)

    loads = [
        pltpu.make_async_copy(pot, a_ext.at[:, pl.ds(B, rows), :], load_sem.at[0]),
        pltpu.make_async_copy(cur, c_ext.at[:, pl.ds(B, rows), :], load_sem.at[1]),
        pltpu.make_async_copy(mat, m_ext.at[:, pl.ds(B, rows), :], load_sem.at[2]),
    ]
    small = [
        pltpu.make_async_copy(src, dst, load_sem.at[3 + i])
        for i, (src, dst) in enumerate(
            ((flux_hbm, flux), (jitter_hbm, jitter), (nu_hbm, nu), (sat_hbm, sat)))
    ]
    for load in small + loads:
        load.start()

    bar = pltpu.get_barrier_semaphore()
    prev, nxt = (az + n_az - 1) % n_az, (az + 1) % n_az

    def greet(who):
        pl.semaphore_signal(bar, inc=1, device_id=who, device_id_type=MESH)

    greet((prev, rad))
    greet((nxt, rad))

    @pl.when(has_left)
    def _():
        greet((az, rad - 1))

    @pl.when(has_right)
    def _():
        greet((az, rad + 1))

    window = [(dz, dx) for dz in (-2, -1, 0, 1, 2) for dx in (0, 1) if (dz, dx) != (0, 0)]

    @pl.when(gap)
    def _():
        for dz, dx in window:
            greet(place(dz, dx))

        @pl.when(az != 0)
        def _():
            greet(place(-3, 0))
            greet(place(3, 0))

        @pl.when(az == 0)
        def _():
            for far in range(3, n_z - 2):
                for side in (0, 1):
                    greet((far * 2 + side, rad))

    up_ok = jnp.logical_not((z == n_z - 3) & (x == 0))
    down_ok = jnp.logical_not((z == 3) & (x == 0))
    one = lambda flag: jnp.where(flag, 1, 0).astype(jnp.int32)
    expected = 2 + one(has_left) + one(has_right)
    expected = expected + one(gap) * (len(window) + one(up_ok) + one(down_ok)) + one(direct)

    for load in small:
        load.wait()
    half = rows // 2
    block[0:8, :] = flux[0:8, 0:half]
    block[8:16, :] = flux[0:8, half:rows]
    block[16:17, :] = flux[8:9, 0:half]
    block[17:18, :] = flux[8:9, half:rows]
    for part in (0, 1):
        turned = offset[0] + jitter[pl.ds(part * half, half)].reshape(1, half)
        turned = jnp.where(turned >= cells, turned - cells, turned)
        block[18 + part : 19 + part, :] = turned.astype(F32)
    block[20:24, :] = jnp.zeros((4, half), F32)

    stacked[...] = jnp.zeros_like(stacked)

    for buf, count in ((a_ext, NF), (c_ext, NF), (m_ext, L)):
        for i in range(count):
            buf[i, 0:B, :] = jnp.zeros((B, LANES), buf.dtype)
            buf[i, B + rows : B + rows + B, :] = jnp.zeros((B, LANES), buf.dtype)

    for f in range(NF):
        s_c[f, 0:2, :] = jnp.zeros((2, STRIP), F32)
        s_c[f, 13:16, :] = jnp.zeros((3, STRIP), F32)
    for l in range(L):
        s_m[l, 15:16, :] = jnp.zeros((1, STRIP), F32)

    for load in loads:
        load.wait()
    last = B + rows
    for f in range(NF):
        to_prev[3 * f : 3 * f + 3, :] = a_ext[f, B : B + 3, :]
        to_prev[33 + f : 34 + f, :] = c_ext[f, B : B + 1, :]
        to_next[2 * f : 2 * f + 2, :] = a_ext[f, last - 2 : last, :]
        to_next[24 + f : 25 + f, :] = c_ext[f, last - 1 : last, :]
    for l in range(L):
        to_prev[27 + 2 * l : 29 + 2 * l, :] = m_ext[l, B : B + 2, :].astype(F32)
        to_next[18 + 2 * l : 20 + 2 * l, :] = m_ext[l, last - 2 : last, :].astype(F32)
    to_prev[42:48, :] = jnp.zeros((6, LANES), F32)
    to_next[33:40, :] = jnp.zeros((7, LANES), F32)

    nu_half = [nu[i] * 0.5 for i in range(MAT)]
    sat_of = [sat[i] for i in range(MAT)]

    def faces_of(q, q_next, q_prev, q_right, q_left, q_above, q_below):
        faces = [q + q_next, q + q_prev, q + q_right, q + q_left]
        faces.append(q if q_above is None else q + q_above)
        faces.append(q if q_below is None else q + q_below)
        return faces

    def main_faces(e, n, l):
        q = q_ext[l, pl.ds(e, n), :]
        return faces_of(
            q, q_ext[l, pl.ds(e + 1, n), :], q_ext[l, pl.ds(e - 1, n), :],
            pltpu.roll(q, LANES - 1, 1), pltpu.roll(q, 1, 1),
            q_ext[l + 1, pl.ds(e, n), :] if l + 1 < L else None, q_ext[l - 1, pl.ds(e, n), :] if l > 0 else None)

    def main_neighbours(field, e, n, c, l):
        here = field[c * L + l, pl.ds(e, n), :]
        return [
            field[c * L + l, pl.ds(e + 1, n), :], field[c * L + l, pl.ds(e - 1, n), :],
            pltpu.roll(here, LANES - 1, 1), pltpu.roll(here, 1, 1),
            field[c * L + l + 1, pl.ds(e, n), :] if l + 1 < L else None,
            field[c * L + l - 1, pl.ds(e, n), :] if l > 0 else None]

    def reluct_rows(e, n):
        for l in range(L):
            flux_sq = jnp.zeros((n, LANES), F32)
            for c in range(3):
                here = a_ext[c * L + l, pl.ds(e, n), :]
                along = a_ext[c * L + l, pl.ds(e + 1, n), :] - here
                across = pltpu.roll(here, LANES - 1, 1) - here
                flux_sq = flux_sq + along * along + across * across
            q_ext[l, pl.ds(e, n), :] = half_reluct(m_ext[l, pl.ds(e, n), :], flux_sq, nu_half, sat_of)

    def first_rows(e, n):
        for l in range(L):
            faces = main_faces(e, n, l)
            inverse = 1.0 / (1.0 + sum(faces[1:], faces[0]))
            inv_ext[l, pl.ds(e, n), :] = inverse
            for c in range(3):
                source = c_ext[c * L + l, pl.ds(e, n), :]
                v_ext[c * L + l, pl.ds(e, n), :] = sweep(main_neighbours(a_ext, e, n, c, l), source, faces, inverse)

    def second_rows(e, n):
        for l in range(L):
            faces = main_faces(e, n, l)
            inverse = inv_ext[l, pl.ds(e, n), :]
            for c in range(3):
                source = c_ext[c * L + l, pl.ds(e, n), :]
                out[c * L + l, pl.ds(e - B, n), :] = sweep(main_neighbours(v_ext, e, n, c, l), source, faces, inverse)

    def outer(step, low, high):
        (low_from, low_to), (high_from, high_to) = low, high
        count_low, count = (low_to - low_from) // 8, (low_to - low_from + high_to - high_from) // 8

        @pl.loop(0, count)
        def _(i):
            jump = jnp.where(i >= count_low, high_from - low_to, 0)
            step(pl.multiple_of(low_from + i * 8 + jump, 8), 8)

    def reluct_inner():
        @pl.loop(0, rows // 16 - 1)
        def _(i):
            reluct_rows(pl.multiple_of(i * 16 + B, 16), 16)

    def reluct_outer():
        outer(reluct_rows, (B - 8, B), (last - 16, last + 8))

    def first_outer():
        outer(first_rows, (B - 8, B + 16), (last - 32, last + 8))

    def second_outer():
        outer(second_rows, (B, B + 32), (last - 48, last))

    def first_inner():
        @pl.loop(0, rows // 16 - 3)
        def _(i):
            first_rows(pl.multiple_of(i * 16 + B + 16, 16), 16)

    def second_inner():
        @pl.loop(0, rows // 16 - 5)
        def _(i):
            second_rows(pl.multiple_of(i * 16 + B + 32, 16), 16)

    def to_strip(f, dst, tile, lanes):
        turned = tile.T
        dst[f, 2:8, lanes] = turned[0:6]
        dst[f, 8:13, lanes] = turned[LANES - 5 : LANES]

    def pack(count, lanes, left, right):
        for f in range(NF):
            left[3 * f : 3 * f + 3, :] = s_a[f, 2:5, lanes]
            left[33 + f : 34 + f, :] = s_c[f, 2:3, lanes]
            right[2 * f : 2 * f + 2, :] = s_a[f, 11:13, lanes]
            right[24 + f : 25 + f, :] = s_c[f, 12:13, lanes]
        for l in range(L):
            left[27 + 2 * l : 29 + 2 * l, :] = s_m[l, 2:4, lanes]
            right[18 + 2 * l : 20 + 2 * l, :] = s_m[l, 11:13, lanes]
        left[42:48, :] = jnp.zeros((6, count), F32)
        right[33:40, :] = jnp.zeros((7, count), F32)

    def columns():
        @pl.loop(0, NF)
        def _(f):
            for part in (0, 1):
                lanes = slice(part * LANES, (part + 1) * LANES)
                to_strip(f, s_a, a_ext[f, B + part * LANES : B + (part + 1) * LANES, :], lanes)
                to_strip(f, s_c, c_ext[f, B + part * LANES : B + (part + 1) * LANES, :], lanes)

        @pl.loop(0, L)
        def _(l):
            for part in (0, 1):
                lanes = slice(part * LANES, (part + 1) * LANES)
                to_strip(l, s_m, m_ext[l, B + part * LANES : B + (part + 1) * LANES, :].astype(F32), lanes)

        pack(rows, slice(0, rows), left_main, right_main)

    early = az == 0

    @pl.when(early)
    def _():
        columns()
        reluct_inner()
        first_inner()
        second_inner()

    pl.semaphore_wait(bar, expected)

    def panels(src, dst, send, recv, who):
        return pltpu.make_async_remote_copy(
            src_ref=src, dst_ref=dst, send_sem=pan_send.at[send], recv_sem=pan_recv.at[recv],
            device_id=who, device_id_type=MESH)

    def direct_copy(recv):
        return panels(block, land.at[slot_k * 2 + x], 9, recv, (0, rad))

    window_copies = [
        panels(block, land.at[(8 - dz) * 2 + x], i, 0, place(dz, dx)) for i, (dz, dx) in enumerate(window)
    ]
    own_copy = pltpu.make_async_copy(block, land.at[16 + x], pan_recv.at[0])
    far_regions = ((1, 3, 6), (2, 11, 14), (3, 0, 3), (4, 14, 16))

    @pl.when(gap)
    def _():
        for recv, low, high in far_regions:

            @pl.when(direct & (slot_k >= low) & (slot_k < high))
            def _():
                direct_copy(recv).start()

        for copy in window_copies:
            copy.start()
        own_copy.start()

    def az_copy(src, dst, i, who):
        return pltpu.make_async_remote_copy(
            src_ref=src, dst_ref=dst, send_sem=az_send.at[i], recv_sem=az_recv.at[i],
            device_id=(who, rad), device_id_type=MESH)

    down_copy = az_copy(to_prev, from_next, 0, prev)
    up_copy = az_copy(to_next, from_prev, 1, nxt)
    down_copy.start()
    up_copy.start()

    def rad_copy(src, dst, i, who):
        return pltpu.make_async_remote_copy(
            src_ref=src, dst_ref=dst, send_sem=rad_send.at[i], recv_sem=rad_recv.at[i],
            device_id=(az, who), device_id_type=MESH)

    left_copies = (rad_copy(left_main, in_right_main, 0, rad - 1), rad_copy(left_corner, in_right_corner, 1, rad - 1))
    right_copies = (rad_copy(right_main, in_left_main, 2, rad + 1), rad_copy(right_corner, in_left_corner, 3, rad + 1))

    def send_strips(i):
        @pl.when(has_left)
        def _():
            left_copies[i].start()

        @pl.when(has_right)
        def _():
            right_copies[i].start()

    @pl.when(jnp.logical_not(early))
    def _():
        columns()

    send_strips(0)

    down_copy.wait()
    up_copy.wait()
    for f in range(NF):
        a_ext[f, last : last + 3, :] = from_next[3 * f : 3 * f + 3, :]
        c_ext[f, last : last + 1, :] = from_next[33 + f : 34 + f, :]
        a_ext[f, B - 2 : B, :] = from_prev[2 * f : 2 * f + 2, :]
        c_ext[f, B - 1 : B, :] = from_prev[24 + f : 25 + f, :]
    for l in range(L):
        m_ext[l, last : last + 2, :] = from_next[27 + 2 * l : 29 + 2 * l, :].astype(jnp.int32)
        m_ext[l, B - 2 : B, :] = from_prev[18 + 2 * l : 20 + 2 * l, :].astype(jnp.int32)

    ends = slice(rows, STRIP)
    fields = [(a_ext, s_a, f) for f in range(NF)] + [(c_ext, s_c, f) for f in range(NF)] + [(m_ext, s_m, l) for l in range(L)]
    for low in range(0, len(fields), 8):
        some = fields[low : low + 8]
        stack = []
        for buf, _, f in some:
            stack += [buf[f, B - 8 : B, :].astype(F32), buf[f, last : last + 8, :].astype(F32)]
        if len(some) < 8:
            stack.append(jnp.zeros((LANES - 16 * len(some), LANES), F32))
        turned = jnp.concatenate(stack, axis=0).T
        for place_in, (_, dst, f) in enumerate(some):
            shift = (LANES - 8 - 16 * place_in) % LANES
            dst[f, 2:8, ends] = pltpu.roll(turned[0:8], shift, 1)[0:6]
            dst[f, 8:13, ends] = pltpu.roll(turned[LANES - 8 : LANES], shift, 1)[3:8]

    pack(LANES, ends, left_corner, right_corner)
    send_strips(1)

    def region(low, high, recv):
        view = land.at[pl.ds(low, high - low)]
        return pltpu.make_async_copy(view, view, pan_recv.at[recv])

    two_up = panels(land.at[pl.ds(12, 6)], land.at[pl.ds(6, 6)], 10, 1, place(3, 0))
    two_down = panels(land.at[pl.ds(16, 6)], land.at[pl.ds(22, 6)], 11, 2, place(-3, 0))
    three_up = panels(land.at[pl.ds(6, 6)], land.at[pl.ds(0, 6)], 12, 3, place(3, 0))
    three_down = panels(land.at[pl.ds(22, 4)], land.at[pl.ds(28, 4)], 13, 4, place(-3, 0))

    def when_start(flag, copy):
        @pl.when(flag)
        def _():
            copy.start()

    @pl.when(gap)
    def _():
        region(12, 22, 0).wait()
        when_start(up_ok, two_up)
        when_start(down_ok, two_down)

    late = jnp.logical_not(early)

    @pl.when(late)
    def _():
        reluct_inner()
        first_inner()

    reluct_outer()
    first_outer()

    @pl.when(gap)
    def _():
        region(6, 12, 1).wait()
        region(22, 28, 2).wait()
        when_start(up_ok, three_up)
        when_start(down_ok, three_down)

    @pl.when(late)
    def _():
        second_inner()

    second_outer()

    def deposit(low, high):
        @pl.loop(low // 2, high // 2)
        def _(pair):
            hits, values = [], []
            for slot in (2 * pair, 2 * pair + 1):
                for part in (0, 1):
                    cell = land[slot, 18 + part : 19 + part, :].astype(jnp.int32) - az * rows
                    cell = jnp.where(cell < 0, cell + cells, cell)
                    ahead = jnp.where(cell < rows + 8, cell, -1)
                    cell = jnp.where(cell >= cells - 8, cell - (cells - 8) + rows + 8, ahead)
                    places = lax.broadcasted_iota(jnp.int32, (rows + 16, half), 0)
                    hits.append(jnp.where(places == cell, 1.0, 0.0).astype(jnp.bfloat16))
                    ninth = land[slot, 16 + part : 17 + part, :]
                    values.append(jnp.concatenate(
                        [land[slot, 8 * part : 8 * part + 8, :], ninth, jnp.zeros((7, half), F32)], axis=0))
            value = jnp.concatenate(values, axis=1)
            first = value.astype(jnp.bfloat16)
            rest = value - first.astype(F32)
            second = rest.astype(jnp.bfloat16)
            third = (rest - second.astype(F32)).astype(jnp.bfloat16)
            acc[...] += lax.dot_general(
                jnp.concatenate(hits, axis=1), jnp.concatenate([first, second, third], axis=0),
                (((1,), (1,)), ((), ())), preferred_element_type=F32)

    @pl.when(gap)
    def _():
        acc[...] = jnp.zeros_like(acc)
        spread[...] = jnp.zeros_like(spread)
        deposit(6, 28)

    @pl.when(has_right)
    def _():
        for i, (came, lanes) in enumerate(((in_right_main, slice(0, rows)), (in_right_corner, ends))):
            rad_copy(left_main if i == 0 else left_corner, came, i, rad + 1).wait_recv()
            for f in range(NF):
                s_a[f, 13:16, lanes] = came[3 * f : 3 * f + 3, :]
                s_c[f, 13:14, lanes] = came[33 + f : 34 + f, :]
            for l in range(L):
                s_m[l, 13:15, lanes] = came[27 + 2 * l : 29 + 2 * l, :]

    @pl.when(has_left)
    def _():
        for i, (came, lanes) in enumerate(((in_left_main, slice(0, rows)), (in_left_corner, ends))):
            rad_copy(right_main if i == 0 else right_corner, came, i + 2, rad - 1).wait_recv()
            for f in range(NF):
                s_a[f, 0:2, lanes] = came[2 * f : 2 * f + 2, :]
                s_c[f, 1:2, lanes] = came[24 + f : 25 + f, :]
            for l in range(L):
                s_m[l, 0:2, lanes] = came[18 + 2 * l : 20 + 2 * l, :]

    @pl.when(jnp.logical_not(has_right))
    def _():
        for f in range(NF):
            s_a[f, 13:16, :] = jnp.zeros((3, STRIP), F32)
        for l in range(L):
            s_m[l, 13:15, :] = jnp.zeros((2, STRIP), F32)

    @pl.when(jnp.logical_not(has_left))
    def _():
        for f in range(NF):
            s_a[f, 0:2, :] = jnp.zeros((2, STRIP), F32)
        for l in range(L):
            s_m[l, 0:2, :] = jnp.zeros((2, STRIP), F32)

    column = lax.broadcasted_iota(jnp.int32, (16, STRIP), 0)
    outside = ((column < 2) & (rad == 0)) | ((column > 12) & (rad == n_rad - 1))
    after = lambda v: pltpu.roll(v, STRIP - 1, 1)
    before = lambda v: pltpu.roll(v, 1, 1)
    right_of = lambda v: pltpu.roll(v, 15, 0)
    left_of = lambda v: pltpu.roll(v, 1, 0)

    for l in range(L):
        flux_sq = jnp.zeros((16, STRIP), F32)
        for c in range(3):
            here = s_a[c * L + l]
            along, across = after(here) - here, right_of(here) - here
            flux_sq = flux_sq + along * along + across * across
        q = half_reluct(s_m[l].astype(jnp.int32), flux_sq, nu_half, sat_of)
        s_q[l] = jnp.where(outside, 0.0, q)

    def strip_faces(l):
        q = s_q[l]
        return faces_of(
            q, after(q), before(q), right_of(q), left_of(q),
            s_q[l + 1] if l + 1 < L else None, s_q[l - 1] if l > 0 else None)

    def strip_neighbours(field, c, l):
        here = field[c * L + l]
        return [
            after(here), before(here), right_of(here), left_of(here),
            field[c * L + l + 1] if l + 1 < L else None, field[c * L + l - 1] if l > 0 else None]

    for l in range(L):
        faces = strip_faces(l)
        inverse = 1.0 / (1.0 + sum(faces[1:], faces[0]))
        s_inv[l] = inverse
        for c in range(3):
            swept = sweep(strip_neighbours(s_a, c, l), s_c[c * L + l], faces, inverse)
            s_v[c * L + l] = jnp.where(outside, 0.0, swept)

    @pl.when(gap)
    def _():
        region(0, 6, 3).wait()
        region(28, 32, 4).wait()
        deposit(0, 6)
        deposit(28, 32)
        spread[0 : rows + 8, 0:48] = acc[0 : rows + 8, :]
        spread[STRIP - 8 : STRIP, 0:48] = acc[rows + 8 : rows + 16, :]
        turned = jnp.concatenate(
            [spread[i * LANES : (i + 1) * LANES, :].T for i in range(3)], axis=1
        )
        airgap = turned[0:16] + turned[16:32] + turned[32:48]

        @pl.when(rad == stator)
        def _():
            for f in range(NF):
                row = airgap[f : f + 1]
                s_c[f, 2:3, :] = s_c[f, 2:3, :] + row
                s_v[f, 2:3, :] = s_v[f, 2:3, :] + row * s_inv[f % L, 2:3, :]

        @pl.when(rad == stator - 1)
        def _():
            for f in range(NF):
                s_v[f, 13:14, :] = s_v[f, 13:14, :] + airgap[f : f + 1] * s_inv[f % L, 13:14, :]

    lane = lax.broadcasted_iota(jnp.int32, (LANES, LANES), 1)
    edge = (lane < 2) | (lane > LANES - 4)
    for l in range(L):
        faces = strip_faces(l)
        for c in range(3):
            f = c * L + l
            done = sweep(strip_neighbours(s_v, c, l), s_c[f], faces, s_inv[l])
            stacked[8 * f : 8 * f + 3, :] = done[10:13, 0:rows]
            stacked[8 * f + 3 : 8 * f + 5, :] = done[2:4, 0:rows]
    for part in (0, 1):
        here = slice(part * LANES, (part + 1) * LANES)
        turned = stacked[:, here].T
        for f in range(NF):
            out[f, here, :] = jnp.where(edge, pltpu.roll(turned, (LANES - 3 - 8 * f) % LANES, 1), out[f, here, :])

    for i in (0, 1):
        @pl.when(has_left)
        def _():
            left_copies[i].wait_send()

        @pl.when(has_right)
        def _():
            right_copies[i].wait_send()

    @pl.when(gap)
    def _():
        for copy in window_copies:
            copy.wait_send()

        @pl.when(direct)
        def _():
            direct_copy(1).wait_send()

        @pl.when(up_ok)
        def _():
            two_up.wait_send()
            three_up.wait_send()

        @pl.when(down_ok)
        def _():
            two_down.wait_send()
            three_down.wait_send()


def local(potential, current, material, nu_table, sat_table, panel_flux, panel_jitter, rotor_offset):
    rows, lanes = potential.shape[2:]
    vmem = lambda *shape: pltpu.VMEM(shape, F32)
    tall = rows + 2 * B
    hbm = pl.BlockSpec(memory_space=pltpu.HBM)
    whole = pl.BlockSpec(memory_space=pltpu.VMEM)
    result = pl.pallas_call(
        kernel,
        out_shape=jax.ShapeDtypeStruct((NF, rows, lanes), F32),
        in_specs=[hbm] * 7 + [pl.BlockSpec(memory_space=pltpu.SMEM)],
        out_specs=whole,
        scratch_shapes=[
            pltpu.SMEM((MAT,), F32), pltpu.SMEM((MAT,), F32), vmem(*panel_flux.shape),
            pltpu.VMEM(panel_jitter.shape, jnp.int32),
            vmem(NF, tall, lanes), vmem(NF, tall, lanes), pltpu.VMEM((L, tall, lanes), jnp.int32),
            vmem(L, tall, lanes), vmem(L, tall, lanes), vmem(NF, tall, lanes),
            vmem(TO_LEFT, lanes), vmem(TO_RIGHT, lanes), vmem(TO_RIGHT, lanes), vmem(TO_LEFT, lanes),
            vmem(TO_LEFT, rows), vmem(TO_LEFT, LANES), vmem(TO_RIGHT, rows), vmem(TO_RIGHT, LANES),
            vmem(TO_LEFT, rows), vmem(TO_LEFT, LANES), vmem(TO_RIGHT, rows), vmem(TO_RIGHT, LANES),
            vmem(NF, 16, STRIP), vmem(L, 16, STRIP), vmem(NF, 16, STRIP),
            vmem(L, 16, STRIP), vmem(L, 16, STRIP), vmem(NF, 16, STRIP),
            vmem(24, LANES), vmem(32, 24, LANES), vmem(rows + 16, 48), vmem(STRIP, LANES), vmem(LANES, rows),
            pltpu.SemaphoreType.DMA((7,)), pltpu.SemaphoreType.DMA((2,)), pltpu.SemaphoreType.DMA((2,)),
            pltpu.SemaphoreType.DMA((4,)), pltpu.SemaphoreType.DMA((4,)),
            pltpu.SemaphoreType.DMA((14,)), pltpu.SemaphoreType.DMA((5,)),
        ],
        compiler_params=pltpu.CompilerParams(
            collective_id=0, has_side_effects=True, vmem_limit_bytes=48 * 1024 * 1024
        ),
    )(
        *[
            pltpu.with_memory_space_constraint(v, pltpu.HBM)
            for v in (
                potential.reshape(NF, rows, lanes), current.reshape(NF, rows, lanes), material,
                nu_table, sat_table, panel_flux, panel_jitter)
        ],
        rotor_offset,
    )
    return result.reshape(potential.shape)


def solution(mesh):
    placed = (
        P(None, None, "az", "rad"),
        P(None, None, "az", "rad"),
        P(None, "az", "rad"),
        P(),
        P(),
        P(None, "az"),
        P("az"),
        P(),
    )
    return jax.shard_map(
        local, mesh=mesh, in_specs=placed, out_specs=P(None, None, "az", "rad"), check_vma=False
    )
```

```python
import jax
import jax.numpy as jnp
from jax import lax
from jax.experimental import pallas as pl
from jax.experimental.pallas import tpu as pltpu
from jax.sharding import PartitionSpec as P

MESH = pl.DeviceIdType.MESH
F32 = jnp.float32
L, NF, MAT = 3, 9, 8
SERVED = 1
B = 16
LANES = 128
STRIP = 384
TO_LEFT, TO_RIGHT = 48, 40


def lookup(material, table):
    low, mid, high = [(material & bit) != 0 for bit in (1, 2, 4)]
    pairs = [jnp.where(low, table[2 * i + 1], table[2 * i]) for i in range(4)]
    quads = [jnp.where(mid, pairs[2 * i + 1], pairs[2 * i]) for i in range(2)]
    return jnp.where(high, quads[1], quads[0])


def half_reluct(material, flux_sq, nu_half, sat):
    return lookup(material, nu_half) * (1.0 + lookup(material, sat) * flux_sq / (1.0 + flux_sq))


def sweep(values, source, faces, inverse):
    total = source
    for face, value in zip(faces, values):
        if value is not None:
            total = total + face * value
    return total * inverse


def kernel(
    pot, cur, mat, nu_hbm, sat_hbm, flux_hbm, jitter_hbm, offset, out,
    nu, sat, flux, jitter,
    a_ext, c_ext, m_ext, q_ext, inv_ext, v_ext,
    to_prev, to_next, from_prev, from_next,
    left_main, left_corner, right_main, right_corner,
    in_right_main, in_right_corner, in_left_main, in_left_corner,
    s_a, s_m, s_c, s_q, s_inv, s_v,
    block, land, acc, spread, stacked, part_out, part_in,
    load_sem, az_send, az_recv, rad_send, rad_recv, pan_send, pan_recv,
):
    az, rad = lax.axis_index("az"), lax.axis_index("rad")
    n_az, n_rad = lax.axis_size("az"), lax.axis_size("rad")
    n_z = n_az // 2
    rows = pot.shape[1]
    cells = rows * n_az
    z, x = az // 2, az % 2
    stator = n_rad // 2
    gap = (rad == stator) | (rad == stator - 1)
    has_left, has_right = rad > 0, rad < n_rad - 1
    served = [(z_to, x_to) for z_to in range(SERVED) for x_to in (0, 1)]
    slots = [(z - z_to + n_z // 2 + n_z) % n_z for z_to, _ in served]
    direct = [gap & ((k < 6) | (k > 10)) for k in slots]

    def place(dz, dx):
        return (((z + dz + n_z) % n_z) * 2 + (x + dx) % 2, rad)

    loads = [
        pltpu.make_async_copy(pot, a_ext.at[:, pl.ds(B, rows), :], load_sem.at[0]),
        pltpu.make_async_copy(cur, c_ext.at[:, pl.ds(B, rows), :], load_sem.at[1]),
        pltpu.make_async_copy(mat, m_ext.at[:, pl.ds(B, rows), :], load_sem.at[2]),
    ]
    small = [
        pltpu.make_async_copy(src, dst, load_sem.at[3 + i])
        for i, (src, dst) in enumerate(
            ((flux_hbm, flux), (jitter_hbm, jitter), (nu_hbm, nu), (sat_hbm, sat)))
    ]
    for load in small + loads:
        load.start()

    bar = pltpu.get_barrier_semaphore()
    prev, nxt = (az + n_az - 1) % n_az, (az + 1) % n_az

    def greet(who):
        pl.semaphore_signal(bar, inc=1, device_id=who, device_id_type=MESH)

    greet((prev, rad))
    greet((nxt, rad))

    @pl.when(has_left)
    def _():
        greet((az, rad - 1))

    @pl.when(has_right)
    def _():
        greet((az, rad + 1))

    window = [(dz, dx) for dz in (-2, -1, 0, 1, 2) for dx in (0, 1) if (dz, dx) != (0, 0)]

    @pl.when(gap)
    def _():
        for dz, dx in window:
            greet(place(dz, dx))

        @pl.when(z >= SERVED)
        def _():
            greet(place(-3, 0))
            greet(place(3, 0))

        @pl.when(z < SERVED)
        def _():
            for far in range(3, n_z - 2):
                for side in (0, 1):
                    greet((((z + far) % n_z) * 2 + side, rad))

    up_ok = (z + 3) % n_z >= SERVED
    down_ok = (z + n_z - 3) % n_z >= SERVED
    one = lambda flag: jnp.where(flag, 1, 0).astype(jnp.int32)
    expected = 2 + one(has_left) + one(has_right)
    expected = expected + one(gap) * (len(window) + one(up_ok) + one(down_ok)) + sum(one(flag) for flag in direct)

    for load in small:
        load.wait()
    half = rows // 2
    block[0:8, :] = flux[0:8, 0:half]
    block[8:16, :] = flux[0:8, half:rows]
    block[16:17, :] = flux[8:9, 0:half]
    block[17:18, :] = flux[8:9, half:rows]
    for part in (0, 1):
        turned = offset[0] + jitter[pl.ds(part * half, half)].reshape(1, half)
        turned = jnp.where(turned >= cells, turned - cells, turned)
        block[18 + part : 19 + part, :] = turned.astype(F32)

    stacked[...] = jnp.zeros_like(stacked)
    spread[...] = jnp.zeros_like(spread)

    for buf, count in ((a_ext, NF), (c_ext, NF), (m_ext, L)):
        for i in range(count):
            buf[i, 0:B, :] = jnp.zeros((B, LANES), buf.dtype)
            buf[i, B + rows : B + rows + B, :] = jnp.zeros((B, LANES), buf.dtype)

    for f in range(NF):
        s_c[f, 0:2, :] = jnp.zeros((2, STRIP), F32)
        s_c[f, 13:16, :] = jnp.zeros((3, STRIP), F32)
    for l in range(L):
        s_m[l, 15:16, :] = jnp.zeros((1, STRIP), F32)

    for load in loads:
        load.wait()
    last = B + rows
    for f in range(NF):
        to_prev[3 * f : 3 * f + 3, :] = a_ext[f, B : B + 3, :]
        to_prev[33 + f : 34 + f, :] = c_ext[f, B : B + 1, :]
        to_next[2 * f : 2 * f + 2, :] = a_ext[f, last - 2 : last, :]
        to_next[24 + f : 25 + f, :] = c_ext[f, last - 1 : last, :]
    for l in range(L):
        to_prev[27 + 2 * l : 29 + 2 * l, :] = m_ext[l, B : B + 2, :].astype(F32)
        to_next[18 + 2 * l : 20 + 2 * l, :] = m_ext[l, last - 2 : last, :].astype(F32)
    to_prev[42:48, :] = jnp.zeros((6, LANES), F32)
    to_next[33:40, :] = jnp.zeros((7, LANES), F32)

    nu_half = [nu[i] * 0.5 for i in range(MAT)]
    sat_of = [sat[i] for i in range(MAT)]

    def faces_of(q, q_next, q_prev, q_right, q_left, q_above, q_below):
        faces = [q + q_next, q + q_prev, q + q_right, q + q_left]
        faces.append(q if q_above is None else q + q_above)
        faces.append(q if q_below is None else q + q_below)
        return faces

    def main_faces(e, n, l):
        q = q_ext[l, pl.ds(e, n), :]
        return faces_of(
            q, q_ext[l, pl.ds(e + 1, n), :], q_ext[l, pl.ds(e - 1, n), :],
            pltpu.roll(q, LANES - 1, 1), pltpu.roll(q, 1, 1),
            q_ext[l + 1, pl.ds(e, n), :] if l + 1 < L else None, q_ext[l - 1, pl.ds(e, n), :] if l > 0 else None)

    def main_neighbours(field, e, n, c, l):
        here = field[c * L + l, pl.ds(e, n), :]
        return [
            field[c * L + l, pl.ds(e + 1, n), :], field[c * L + l, pl.ds(e - 1, n), :],
            pltpu.roll(here, LANES - 1, 1), pltpu.roll(here, 1, 1),
            field[c * L + l + 1, pl.ds(e, n), :] if l + 1 < L else None,
            field[c * L + l - 1, pl.ds(e, n), :] if l > 0 else None]

    def reluct_rows(e, n):
        for l in range(L):
            flux_sq = jnp.zeros((n, LANES), F32)
            for c in range(3):
                here = a_ext[c * L + l, pl.ds(e, n), :]
                along = a_ext[c * L + l, pl.ds(e + 1, n), :] - here
                across = pltpu.roll(here, LANES - 1, 1) - here
                flux_sq = flux_sq + along * along + across * across
            q_ext[l, pl.ds(e, n), :] = half_reluct(m_ext[l, pl.ds(e, n), :], flux_sq, nu_half, sat_of)

    def first_rows(e, n):
        for l in range(L):
            faces = main_faces(e, n, l)
            inverse = 1.0 / (1.0 + sum(faces[1:], faces[0]))
            inv_ext[l, pl.ds(e, n), :] = inverse
            for c in range(3):
                source = c_ext[c * L + l, pl.ds(e, n), :]
                v_ext[c * L + l, pl.ds(e, n), :] = sweep(main_neighbours(a_ext, e, n, c, l), source, faces, inverse)

    def second_rows(e, n):
        for l in range(L):
            faces = main_faces(e, n, l)
            inverse = inv_ext[l, pl.ds(e, n), :]
            for c in range(3):
                source = c_ext[c * L + l, pl.ds(e, n), :]
                out[c * L + l, pl.ds(e - B, n), :] = sweep(main_neighbours(v_ext, e, n, c, l), source, faces, inverse)

    def outer(step, low, high):
        (low_from, low_to), (high_from, high_to) = low, high
        count_low, count = (low_to - low_from) // 8, (low_to - low_from + high_to - high_from) // 8

        @pl.loop(0, count)
        def _(i):
            jump = jnp.where(i >= count_low, high_from - low_to, 0)
            step(pl.multiple_of(low_from + i * 8 + jump, 8), 8)

    def reluct_inner():
        @pl.loop(0, rows // 16 - 1)
        def _(i):
            reluct_rows(pl.multiple_of(i * 16 + B, 16), 16)

    def reluct_outer():
        outer(reluct_rows, (B - 8, B), (last - 16, last + 8))

    def first_outer():
        outer(first_rows, (B - 8, B + 16), (last - 32, last + 8))

    def second_outer():
        outer(second_rows, (B, B + 32), (last - 48, last))

    def first_inner():
        @pl.loop(0, rows // 16 - 3)
        def _(i):
            first_rows(pl.multiple_of(i * 16 + B + 16, 16), 16)

    def second_inner():
        @pl.loop(0, rows // 16 - 5)
        def _(i):
            second_rows(pl.multiple_of(i * 16 + B + 32, 16), 16)

    def to_strip(f, dst, tile, lanes):
        turned = tile.T
        dst[f, 2:8, lanes] = turned[0:6]
        dst[f, 8:13, lanes] = turned[LANES - 5 : LANES]

    def pack(count, lanes, left, right):
        for f in range(NF):
            left[3 * f : 3 * f + 3, :] = s_a[f, 2:5, lanes]
            left[33 + f : 34 + f, :] = s_c[f, 2:3, lanes]
            right[2 * f : 2 * f + 2, :] = s_a[f, 11:13, lanes]
            right[24 + f : 25 + f, :] = s_c[f, 12:13, lanes]
        for l in range(L):
            left[27 + 2 * l : 29 + 2 * l, :] = s_m[l, 2:4, lanes]
            right[18 + 2 * l : 20 + 2 * l, :] = s_m[l, 11:13, lanes]
        left[42:48, :] = jnp.zeros((6, count), F32)
        right[33:40, :] = jnp.zeros((7, count), F32)

    def columns():
        @pl.loop(0, NF)
        def _(f):
            for part in (0, 1):
                lanes = slice(part * LANES, (part + 1) * LANES)
                to_strip(f, s_a, a_ext[f, B + part * LANES : B + (part + 1) * LANES, :], lanes)
                to_strip(f, s_c, c_ext[f, B + part * LANES : B + (part + 1) * LANES, :], lanes)

        @pl.loop(0, L)
        def _(l):
            for part in (0, 1):
                lanes = slice(part * LANES, (part + 1) * LANES)
                to_strip(l, s_m, m_ext[l, B + part * LANES : B + (part + 1) * LANES, :].astype(F32), lanes)

        pack(rows, slice(0, rows), left_main, right_main)

    early = (gap & (z < 4)) | (az == 0)

    @pl.when(early)
    def _():
        columns()
        reluct_inner()
        first_inner()
        second_inner()

    pl.semaphore_wait(bar, expected)

    def panels(src, dst, send, recv, who):
        return pltpu.make_async_remote_copy(
            src_ref=src, dst_ref=dst, send_sem=pan_send.at[send], recv_sem=pan_recv.at[recv],
            device_id=who, device_id_type=MESH)

    def direct_copy(i, recv):
        z_to, x_to = served[i]
        return panels(block, land.at[slots[i] * 2 + x], 14 + i, recv, (z_to * 2 + x_to, rad))

    window_copies = [
        panels(block, land.at[(8 - dz) * 2 + x], i, 0, place(dz, dx)) for i, (dz, dx) in enumerate(window)
    ]
    own_copy = pltpu.make_async_copy(block, land.at[16 + x], pan_recv.at[0])
    far_regions = ((1, 3, 6), (2, 11, 14), (3, 0, 3), (4, 14, 16))

    @pl.when(gap)
    def _():
        for i, k in enumerate(slots):
            for recv, low, high in far_regions:

                @pl.when((k >= low) & (k < high))
                def _():
                    direct_copy(i, recv).start()

        for copy in window_copies:
            copy.start()
        own_copy.start()

    def az_copy(src, dst, i, who):
        return pltpu.make_async_remote_copy(
            src_ref=src, dst_ref=dst, send_sem=az_send.at[i], recv_sem=az_recv.at[i],
            device_id=(who, rad), device_id_type=MESH)

    down_copy = az_copy(to_prev, from_next, 0, prev)
    up_copy = az_copy(to_next, from_prev, 1, nxt)
    down_copy.start()
    up_copy.start()

    def rad_copy(src, dst, i, who):
        return pltpu.make_async_remote_copy(
            src_ref=src, dst_ref=dst, send_sem=rad_send.at[i], recv_sem=rad_recv.at[i],
            device_id=(az, who), device_id_type=MESH)

    left_copies = (rad_copy(left_main, in_right_main, 0, rad - 1), rad_copy(left_corner, in_right_corner, 1, rad - 1))
    right_copies = (rad_copy(right_main, in_left_main, 2, rad + 1), rad_copy(right_corner, in_left_corner, 3, rad + 1))

    def send_strips(i):
        @pl.when(has_left)
        def _():
            left_copies[i].start()

        @pl.when(has_right)
        def _():
            right_copies[i].start()

    @pl.when(jnp.logical_not(early))
    def _():
        columns()

    send_strips(0)

    down_copy.wait()
    up_copy.wait()
    for f in range(NF):
        a_ext[f, last : last + 3, :] = from_next[3 * f : 3 * f + 3, :]
        c_ext[f, last : last + 1, :] = from_next[33 + f : 34 + f, :]
        a_ext[f, B - 2 : B, :] = from_prev[2 * f : 2 * f + 2, :]
        c_ext[f, B - 1 : B, :] = from_prev[24 + f : 25 + f, :]
    for l in range(L):
        m_ext[l, last : last + 2, :] = from_next[27 + 2 * l : 29 + 2 * l, :].astype(jnp.int32)
        m_ext[l, B - 2 : B, :] = from_prev[18 + 2 * l : 20 + 2 * l, :].astype(jnp.int32)

    ends = slice(rows, STRIP)
    fields = [(a_ext, s_a, f) for f in range(NF)] + [(c_ext, s_c, f) for f in range(NF)] + [(m_ext, s_m, l) for l in range(L)]
    for low in range(0, len(fields), 8):
        some = fields[low : low + 8]
        stack = []
        for buf, _, f in some:
            stack += [buf[f, B - 8 : B, :].astype(F32), buf[f, last : last + 8, :].astype(F32)]
        if len(some) < 8:
            stack.append(jnp.zeros((LANES - 16 * len(some), LANES), F32))
        turned = jnp.concatenate(stack, axis=0).T
        for place_in, (_, dst, f) in enumerate(some):
            shift = (LANES - 8 - 16 * place_in) % LANES
            dst[f, 2:8, ends] = pltpu.roll(turned[0:8], shift, 1)[0:6]
            dst[f, 8:13, ends] = pltpu.roll(turned[LANES - 8 : LANES], shift, 1)[3:8]

    pack(LANES, ends, left_corner, right_corner)
    send_strips(1)

    def region(low, high, recv):
        view = land.at[pl.ds(low, high - low)]
        return pltpu.make_async_copy(view, view, pan_recv.at[recv])

    two_up = panels(land.at[pl.ds(12, 6)], land.at[pl.ds(6, 6)], 10, 1, place(3, 0))
    two_down = panels(land.at[pl.ds(16, 6)], land.at[pl.ds(22, 6)], 11, 2, place(-3, 0))
    part_up = panels(part_out.at[0], part_in.at[0], 12, 3, place(3, 0))
    part_down = panels(part_out.at[1], part_in.at[1], 13, 4, place(-3, 0))

    def when_start(flag, copy):
        @pl.when(flag)
        def _():
            copy.start()

    @pl.when(gap)
    def _():
        region(12, 22, 0).wait()
        when_start(up_ok, two_up)
        when_start(down_ok, two_down)

    late = jnp.logical_not(early)

    @pl.when(late)
    def _():
        reluct_inner()
        first_inner()

    reluct_outer()
    first_outer()

    def deposit(low, high, tile):
        @pl.loop(low // 2, high // 2)
        def _(pair):
            hits, values = [], []
            for slot in (2 * pair, 2 * pair + 1):
                for part in (0, 1):
                    cell = land[slot, 18 + part : 19 + part, :].astype(jnp.int32) - tile * rows
                    cell = jnp.where(cell < 0, cell + cells, cell)
                    ahead = jnp.where(cell < rows + 8, cell, -1)
                    cell = jnp.where(cell >= cells - 8, cell - (cells - 8) + rows + 8, ahead)
                    places = lax.broadcasted_iota(jnp.int32, (rows + 16, half), 0)
                    hits.append(jnp.where(places == cell, 1.0, 0.0).astype(jnp.bfloat16))
                    ninth = land[slot, 16 + part : 17 + part, :]
                    values.append(jnp.concatenate(
                        [land[slot, 8 * part : 8 * part + 8, :], ninth, jnp.zeros((7, half), F32)], axis=0))
            value = jnp.concatenate(values, axis=1)
            first = value.astype(jnp.bfloat16)
            rest = value - first.astype(F32)
            second = rest.astype(jnp.bfloat16)
            third = (rest - second.astype(F32)).astype(jnp.bfloat16)
            acc[...] += lax.dot_general(
                jnp.concatenate([first, second, third], axis=0), jnp.concatenate(hits, axis=1),
                (((1,), (1,)), ((), ())), preferred_element_type=F32)

    def deposited():
        return acc[0:NF, :] + acc[16 : 16 + NF, :] + acc[32 : 32 + NF, :]

    def pass_on(flag, i, low, high, dz, copy):
        @pl.when(flag)
        def _():
            acc[...] = jnp.zeros_like(acc)
            deposit(low, high, (z + dz + n_z) % n_z * 2 + x)
            part_out[i] = deposited()
            copy.start()

    @pl.when(gap)
    def _():
        region(6, 12, 1).wait()
        pass_on(up_ok, 0, 6, 12, 3, part_up)
        region(22, 28, 2).wait()
        pass_on(down_ok, 1, 22, 26, -3, part_down)

    @pl.when(late)
    def _():
        second_inner()

    second_outer()

    @pl.when(gap)
    def _():
        acc[...] = jnp.zeros_like(acc)
        deposit(6, 28, az)

    @pl.when(has_right)
    def _():
        for i, (came, lanes) in enumerate(((in_right_main, slice(0, rows)), (in_right_corner, ends))):
            rad_copy(left_main if i == 0 else left_corner, came, i, rad + 1).wait_recv()
            for f in range(NF):
                s_a[f, 13:16, lanes] = came[3 * f : 3 * f + 3, :]
                s_c[f, 13:14, lanes] = came[33 + f : 34 + f, :]
            for l in range(L):
                s_m[l, 13:15, lanes] = came[27 + 2 * l : 29 + 2 * l, :]

    @pl.when(has_left)
    def _():
        for i, (came, lanes) in enumerate(((in_left_main, slice(0, rows)), (in_left_corner, ends))):
            rad_copy(right_main if i == 0 else right_corner, came, i + 2, rad - 1).wait_recv()
            for f in range(NF):
                s_a[f, 0:2, lanes] = came[2 * f : 2 * f + 2, :]
                s_c[f, 1:2, lanes] = came[24 + f : 25 + f, :]
            for l in range(L):
                s_m[l, 0:2, lanes] = came[18 + 2 * l : 20 + 2 * l, :]

    @pl.when(jnp.logical_not(has_right))
    def _():
        for f in range(NF):
            s_a[f, 13:16, :] = jnp.zeros((3, STRIP), F32)
        for l in range(L):
            s_m[l, 13:15, :] = jnp.zeros((2, STRIP), F32)

    @pl.when(jnp.logical_not(has_left))
    def _():
        for f in range(NF):
            s_a[f, 0:2, :] = jnp.zeros((2, STRIP), F32)
        for l in range(L):
            s_m[l, 0:2, :] = jnp.zeros((2, STRIP), F32)

    column = lax.broadcasted_iota(jnp.int32, (16, STRIP), 0)
    outside = ((column < 2) & (rad == 0)) | ((column > 12) & (rad == n_rad - 1))
    after = lambda v: pltpu.roll(v, STRIP - 1, 1)
    before = lambda v: pltpu.roll(v, 1, 1)
    right_of = lambda v: pltpu.roll(v, 15, 0)
    left_of = lambda v: pltpu.roll(v, 1, 0)

    for l in range(L):
        flux_sq = jnp.zeros((16, STRIP), F32)
        for c in range(3):
            here = s_a[c * L + l]
            along, across = after(here) - here, right_of(here) - here
            flux_sq = flux_sq + along * along + across * across
        q = half_reluct(s_m[l].astype(jnp.int32), flux_sq, nu_half, sat_of)
        s_q[l] = jnp.where(outside, 0.0, q)

    def strip_faces(l):
        q = s_q[l]
        return faces_of(
            q, after(q), before(q), right_of(q), left_of(q),
            s_q[l + 1] if l + 1 < L else None, s_q[l - 1] if l > 0 else None)

    def strip_neighbours(field, c, l):
        here = field[c * L + l]
        return [
            after(here), before(here), right_of(here), left_of(here),
            field[c * L + l + 1] if l + 1 < L else None, field[c * L + l - 1] if l > 0 else None]

    for l in range(L):
        faces = strip_faces(l)
        inverse = 1.0 / (1.0 + sum(faces[1:], faces[0]))
        s_inv[l] = inverse
        for c in range(3):
            swept = sweep(strip_neighbours(s_a, c, l), s_c[c * L + l], faces, inverse)
            s_v[c * L + l] = jnp.where(outside, 0.0, swept)

    @pl.when(gap)
    def _():
        @pl.when(z < SERVED)
        def _():
            region(0, 6, 3).wait()
            region(28, 32, 4).wait()
            deposit(0, 6, az)
            deposit(28, 32, az)
            spread[0:NF, 0 : rows + 16] = deposited()

        @pl.when(z >= SERVED)
        def _():
            part_up.wait_recv()
            part_down.wait_recv()
            spread[0:NF, 0 : rows + 16] = deposited() + (part_in[0] + part_in[1])

        summed = spread[...]
        lanes_of = lax.broadcasted_iota(jnp.int32, (16, STRIP), 1)
        airgap = jnp.where(lanes_of >= STRIP - 8, pltpu.roll(summed, STRIP - rows - 16, 1), summed)

        @pl.when(rad == stator)
        def _():
            for f in range(NF):
                row = airgap[f : f + 1]
                s_c[f, 2:3, :] = s_c[f, 2:3, :] + row
                s_v[f, 2:3, :] = s_v[f, 2:3, :] + row * s_inv[f % L, 2:3, :]

        @pl.when(rad == stator - 1)
        def _():
            for f in range(NF):
                s_v[f, 13:14, :] = s_v[f, 13:14, :] + airgap[f : f + 1] * s_inv[f % L, 13:14, :]

    lane = lax.broadcasted_iota(jnp.int32, (LANES, LANES), 1)
    edge = (lane < 2) | (lane > LANES - 4)
    for l in range(L):
        faces = strip_faces(l)
        for c in range(3):
            f = c * L + l
            done = sweep(strip_neighbours(s_v, c, l), s_c[f], faces, s_inv[l])
            stacked[8 * f : 8 * f + 3, :] = done[10:13, 0:rows]
            stacked[8 * f + 3 : 8 * f + 5, :] = done[2:4, 0:rows]
    for part in (0, 1):
        here = slice(part * LANES, (part + 1) * LANES)
        turned = stacked[:, here].T
        for f in range(NF):
            out[f, here, :] = jnp.where(edge, pltpu.roll(turned, (LANES - 3 - 8 * f) % LANES, 1), out[f, here, :])

    for i in (0, 1):
        @pl.when(has_left)
        def _():
            left_copies[i].wait_send()

        @pl.when(has_right)
        def _():
            right_copies[i].wait_send()

    @pl.when(gap)
    def _():
        for copy in window_copies:
            copy.wait_send()

        for i in range(len(served)):

            @pl.when(direct[i])
            def _():
                direct_copy(i, 1).wait_send()

        @pl.when(up_ok)
        def _():
            two_up.wait_send()
            part_up.wait_send()

        @pl.when(down_ok)
        def _():
            two_down.wait_send()
            part_down.wait_send()


def local(potential, current, material, nu_table, sat_table, panel_flux, panel_jitter, rotor_offset):
    rows, lanes = potential.shape[2:]
    vmem = lambda *shape: pltpu.VMEM(shape, F32)
    tall = rows + 2 * B
    hbm = pl.BlockSpec(memory_space=pltpu.HBM)
    whole = pl.BlockSpec(memory_space=pltpu.VMEM)
    result = pl.pallas_call(
        kernel,
        out_shape=jax.ShapeDtypeStruct((NF, rows, lanes), F32),
        in_specs=[hbm] * 7 + [pl.BlockSpec(memory_space=pltpu.SMEM)],
        out_specs=whole,
        scratch_shapes=[
            pltpu.SMEM((MAT,), F32), pltpu.SMEM((MAT,), F32), vmem(*panel_flux.shape),
            pltpu.VMEM(panel_jitter.shape, jnp.int32),
            vmem(NF, tall, lanes), vmem(NF, tall, lanes), pltpu.VMEM((L, tall, lanes), jnp.int32),
            vmem(L, tall, lanes), vmem(L, tall, lanes), vmem(NF, tall, lanes),
            vmem(TO_LEFT, lanes), vmem(TO_RIGHT, lanes), vmem(TO_RIGHT, lanes), vmem(TO_LEFT, lanes),
            vmem(TO_LEFT, rows), vmem(TO_LEFT, LANES), vmem(TO_RIGHT, rows), vmem(TO_RIGHT, LANES),
            vmem(TO_LEFT, rows), vmem(TO_LEFT, LANES), vmem(TO_RIGHT, rows), vmem(TO_RIGHT, LANES),
            vmem(NF, 16, STRIP), vmem(L, 16, STRIP), vmem(NF, 16, STRIP),
            vmem(L, 16, STRIP), vmem(L, 16, STRIP), vmem(NF, 16, STRIP),
            vmem(20, LANES), vmem(32, 20, LANES), vmem(48, rows + 16), vmem(16, STRIP), vmem(LANES, rows),
            vmem(2, NF, rows + 16), vmem(2, NF, rows + 16),
            pltpu.SemaphoreType.DMA((7,)), pltpu.SemaphoreType.DMA((2,)), pltpu.SemaphoreType.DMA((2,)),
            pltpu.SemaphoreType.DMA((4,)), pltpu.SemaphoreType.DMA((4,)),
            pltpu.SemaphoreType.DMA((14 + 2 * SERVED,)), pltpu.SemaphoreType.DMA((5,)),
        ],
        compiler_params=pltpu.CompilerParams(
            collective_id=0, has_side_effects=True, vmem_limit_bytes=48 * 1024 * 1024
        ),
    )(
        *[
            pltpu.with_memory_space_constraint(v, pltpu.HBM)
            for v in (
                potential.reshape(NF, rows, lanes), current.reshape(NF, rows, lanes), material,
                nu_table, sat_table, panel_flux, panel_jitter)
        ],
        rotor_offset,
    )
    return result.reshape(potential.shape)


def solution(mesh):
    placed = (
        P(None, None, "az", "rad"),
        P(None, None, "az", "rad"),
        P(None, "az", "rad"),
        P(),
        P(),
        P(None, "az"),
        P("az"),
        P(),
    )
    return jax.shard_map(
        local, mesh=mesh, in_specs=placed, out_specs=P(None, None, "az", "rad"), check_vma=False
    )
```

```python
import jax
import jax.numpy as jnp
from jax import lax
from jax.experimental import pallas as pl
from jax.experimental.pallas import tpu as pltpu
from jax.sharding import PartitionSpec as P

MESH = pl.DeviceIdType.MESH
F32 = jnp.float32
L, NF, MAT = 3, 9, 8
SERVED = 1
B = 16
LANES = 128
STRIP = 384
TO_LEFT, TO_RIGHT = 48, 40


def lookup(material, table):
    low, mid, high = [(material & bit) != 0 for bit in (1, 2, 4)]
    pairs = [jnp.where(low, table[2 * i + 1], table[2 * i]) for i in range(4)]
    quads = [jnp.where(mid, pairs[2 * i + 1], pairs[2 * i]) for i in range(2)]
    return jnp.where(high, quads[1], quads[0])


def half_reluct(material, flux_sq, nu_half, sat):
    return lookup(material, nu_half) * (1.0 + lookup(material, sat) * flux_sq / (1.0 + flux_sq))


def sweep(values, source, faces, inverse):
    total = source
    for face, value in zip(faces, values):
        if value is not None:
            total = total + face * value
    return total * inverse


def kernel(
    pot, cur, mat, nu_hbm, sat_hbm, flux_hbm, jitter_hbm, offset, out,
    nu, sat, flux, jitter,
    a_ext, c_ext, m_ext, q_ext, inv_ext, v_ext,
    to_prev, to_next, from_prev, from_next,
    left_main, left_corner, right_main, right_corner,
    in_right_main, in_right_corner, in_left_main, in_left_corner,
    s_a, s_m, s_c, s_q, s_inv, s_v,
    block, land, acc, spread, stacked, part_out, part_in,
    load_sem, az_send, az_recv, rad_send, rad_recv, pan_send, pan_recv,
):
    az, rad = lax.axis_index("az"), lax.axis_index("rad")
    n_az, n_rad = lax.axis_size("az"), lax.axis_size("rad")
    n_z = n_az // 2
    rows = pot.shape[1]
    cells = rows * n_az
    z, x = az // 2, az % 2
    stator = n_rad // 2
    gap = (rad == stator) | (rad == stator - 1)
    has_left, has_right = rad > 0, rad < n_rad - 1
    served = [(z_to, x_to) for z_to in range(SERVED) for x_to in (0, 1)]
    slots = [(z - z_to + n_z // 2 + n_z) % n_z for z_to, _ in served]
    direct = [gap & ((k < 6) | (k > 10)) for k in slots]

    def place(dz, dx):
        return (((z + dz + n_z) % n_z) * 2 + (x + dx) % 2, rad)

    loads = [
        pltpu.make_async_copy(pot, a_ext.at[:, pl.ds(B, rows), :], load_sem.at[0]),
        pltpu.make_async_copy(cur, c_ext.at[:, pl.ds(B, rows), :], load_sem.at[1]),
        pltpu.make_async_copy(mat, m_ext.at[:, pl.ds(B, rows), :], load_sem.at[2]),
    ]
    small = [
        pltpu.make_async_copy(src, dst, load_sem.at[3 + i])
        for i, (src, dst) in enumerate(
            ((flux_hbm, flux), (jitter_hbm, jitter), (nu_hbm, nu), (sat_hbm, sat)))
    ]
    for load in small + loads:
        load.start()

    bar = pltpu.get_barrier_semaphore()
    prev, nxt = (az + n_az - 1) % n_az, (az + 1) % n_az

    def greet(who):
        pl.semaphore_signal(bar, inc=1, device_id=who, device_id_type=MESH)

    greet((prev, rad))
    greet((nxt, rad))

    @pl.when(has_left)
    def _():
        greet((az, rad - 1))

    @pl.when(has_right)
    def _():
        greet((az, rad + 1))

    window = [(dz, dx) for dz in (-2, -1, 0, 1, 2) for dx in (0, 1) if (dz, dx) != (0, 0)]

    @pl.when(gap)
    def _():
        for dz, dx in window:
            greet(place(dz, dx))

        @pl.when(z >= SERVED)
        def _():
            greet(place(-3, 0))
            greet(place(3, 0))

        @pl.when(z < SERVED)
        def _():
            for far in range(3, n_z - 2):
                for side in (0, 1):
                    greet((((z + far) % n_z) * 2 + side, rad))

    up_ok = (z + 3) % n_z >= SERVED
    down_ok = (z + n_z - 3) % n_z >= SERVED
    one = lambda flag: jnp.where(flag, 1, 0).astype(jnp.int32)
    expected = 2 + one(has_left) + one(has_right)
    expected = expected + one(gap) * (len(window) + one(up_ok) + one(down_ok)) + sum(one(flag) for flag in direct)

    for load in small:
        load.wait()
    half = rows // 2
    block[0:8, :] = flux[0:8, 0:half]
    block[8:16, :] = flux[0:8, half:rows]
    block[16:17, :] = flux[8:9, 0:half]
    block[17:18, :] = flux[8:9, half:rows]
    for part in (0, 1):
        turned = offset[0] + jitter[pl.ds(part * half, half)].reshape(1, half)
        turned = jnp.where(turned >= cells, turned - cells, turned)
        block[18 + part : 19 + part, :] = turned.astype(F32)

    stacked[...] = jnp.zeros_like(stacked)
    spread[...] = jnp.zeros_like(spread)

    for buf, count in ((a_ext, NF), (c_ext, NF), (m_ext, L)):
        for i in range(count):
            buf[i, 0:B, :] = jnp.zeros((B, LANES), buf.dtype)
            buf[i, B + rows : B + rows + B, :] = jnp.zeros((B, LANES), buf.dtype)

    for f in range(NF):
        s_c[f, 0:2, :] = jnp.zeros((2, STRIP), F32)
        s_c[f, 13:16, :] = jnp.zeros((3, STRIP), F32)
    for l in range(L):
        s_m[l, 15:16, :] = jnp.zeros((1, STRIP), F32)

    for load in loads:
        load.wait()
    last = B + rows
    for f in range(NF):
        to_prev[3 * f : 3 * f + 3, :] = a_ext[f, B : B + 3, :]
        to_prev[33 + f : 34 + f, :] = c_ext[f, B : B + 1, :]
        to_next[2 * f : 2 * f + 2, :] = a_ext[f, last - 2 : last, :]
        to_next[24 + f : 25 + f, :] = c_ext[f, last - 1 : last, :]
    for l in range(L):
        to_prev[27 + 2 * l : 29 + 2 * l, :] = m_ext[l, B : B + 2, :].astype(F32)
        to_next[18 + 2 * l : 20 + 2 * l, :] = m_ext[l, last - 2 : last, :].astype(F32)
    to_prev[42:48, :] = jnp.zeros((6, LANES), F32)
    to_next[33:40, :] = jnp.zeros((7, LANES), F32)

    nu_half = [nu[i] * 0.5 for i in range(MAT)]
    sat_of = [sat[i] for i in range(MAT)]

    def faces_of(q, q_next, q_prev, q_right, q_left, q_above, q_below):
        faces = [q + q_next, q + q_prev, q + q_right, q + q_left]
        faces.append(q if q_above is None else q + q_above)
        faces.append(q if q_below is None else q + q_below)
        return faces

    def main_faces(e, n, l):
        q = q_ext[l, pl.ds(e, n), :]
        return faces_of(
            q, q_ext[l, pl.ds(e + 1, n), :], q_ext[l, pl.ds(e - 1, n), :],
            pltpu.roll(q, LANES - 1, 1), pltpu.roll(q, 1, 1),
            q_ext[l + 1, pl.ds(e, n), :] if l + 1 < L else None, q_ext[l - 1, pl.ds(e, n), :] if l > 0 else None)

    def main_neighbours(field, e, n, c, l):
        here = field[c * L + l, pl.ds(e, n), :]
        return [
            field[c * L + l, pl.ds(e + 1, n), :], field[c * L + l, pl.ds(e - 1, n), :],
            pltpu.roll(here, LANES - 1, 1), pltpu.roll(here, 1, 1),
            field[c * L + l + 1, pl.ds(e, n), :] if l + 1 < L else None,
            field[c * L + l - 1, pl.ds(e, n), :] if l > 0 else None]

    def reluct_rows(e, n):
        for l in range(L):
            flux_sq = jnp.zeros((n, LANES), F32)
            for c in range(3):
                here = a_ext[c * L + l, pl.ds(e, n), :]
                along = a_ext[c * L + l, pl.ds(e + 1, n), :] - here
                across = pltpu.roll(here, LANES - 1, 1) - here
                flux_sq = flux_sq + along * along + across * across
            q_ext[l, pl.ds(e, n), :] = half_reluct(m_ext[l, pl.ds(e, n), :], flux_sq, nu_half, sat_of)

    def first_rows(e, n):
        for l in range(L):
            faces = main_faces(e, n, l)
            inverse = 1.0 / (1.0 + sum(faces[1:], faces[0]))
            inv_ext[l, pl.ds(e, n), :] = inverse
            for c in range(3):
                source = c_ext[c * L + l, pl.ds(e, n), :]
                v_ext[c * L + l, pl.ds(e, n), :] = sweep(main_neighbours(a_ext, e, n, c, l), source, faces, inverse)

    def second_rows(e, n):
        for l in range(L):
            faces = main_faces(e, n, l)
            inverse = inv_ext[l, pl.ds(e, n), :]
            for c in range(3):
                source = c_ext[c * L + l, pl.ds(e, n), :]
                out[c * L + l, pl.ds(e - B, n), :] = sweep(main_neighbours(v_ext, e, n, c, l), source, faces, inverse)

    def outer(step, low, high):
        (low_from, low_to), (high_from, high_to) = low, high
        count_low, count = (low_to - low_from) // 8, (low_to - low_from + high_to - high_from) // 8

        @pl.loop(0, count)
        def _(i):
            jump = jnp.where(i >= count_low, high_from - low_to, 0)
            step(pl.multiple_of(low_from + i * 8 + jump, 8), 8)

    def reluct_inner():
        @pl.loop(0, rows // 16 - 1)
        def _(i):
            reluct_rows(pl.multiple_of(i * 16 + B, 16), 16)

    def reluct_outer():
        outer(reluct_rows, (B - 8, B), (last - 16, last + 8))

    def first_outer():
        outer(first_rows, (B - 8, B + 16), (last - 32, last + 8))

    def second_outer():
        outer(second_rows, (B, B + 32), (last - 48, last))

    def first_inner():
        @pl.loop(0, rows // 16 - 3)
        def _(i):
            first_rows(pl.multiple_of(i * 16 + B + 16, 16), 16)

    def second_inner():
        @pl.loop(0, rows // 16 - 5)
        def _(i):
            second_rows(pl.multiple_of(i * 16 + B + 32, 16), 16)

    def to_strip(f, dst, tile, lanes):
        turned = tile.T
        dst[f, 2:8, lanes] = turned[0:6]
        dst[f, 8:13, lanes] = turned[LANES - 5 : LANES]

    def pack(count, lanes, left, right):
        for f in range(NF):
            left[3 * f : 3 * f + 3, :] = s_a[f, 2:5, lanes]
            left[33 + f : 34 + f, :] = s_c[f, 2:3, lanes]
            right[2 * f : 2 * f + 2, :] = s_a[f, 11:13, lanes]
            right[24 + f : 25 + f, :] = s_c[f, 12:13, lanes]
        for l in range(L):
            left[27 + 2 * l : 29 + 2 * l, :] = s_m[l, 2:4, lanes]
            right[18 + 2 * l : 20 + 2 * l, :] = s_m[l, 11:13, lanes]
        left[42:48, :] = jnp.zeros((6, count), F32)
        right[33:40, :] = jnp.zeros((7, count), F32)

    def columns():
        @pl.loop(0, NF)
        def _(f):
            for part in (0, 1):
                lanes = slice(part * LANES, (part + 1) * LANES)
                to_strip(f, s_a, a_ext[f, B + part * LANES : B + (part + 1) * LANES, :], lanes)
                to_strip(f, s_c, c_ext[f, B + part * LANES : B + (part + 1) * LANES, :], lanes)

        @pl.loop(0, L)
        def _(l):
            for part in (0, 1):
                lanes = slice(part * LANES, (part + 1) * LANES)
                to_strip(l, s_m, m_ext[l, B + part * LANES : B + (part + 1) * LANES, :].astype(F32), lanes)

        pack(rows, slice(0, rows), left_main, right_main)

    early = (gap & (z < 4)) | (az == 0)

    @pl.when(early)
    def _():
        columns()
        reluct_inner()
        first_inner()
        second_inner()

    pl.semaphore_wait(bar, expected)

    def panels(src, dst, send, recv, who):
        return pltpu.make_async_remote_copy(
            src_ref=src, dst_ref=dst, send_sem=pan_send.at[send], recv_sem=pan_recv.at[recv],
            device_id=who, device_id_type=MESH)

    def direct_copy(i, recv):
        z_to, x_to = served[i]
        return panels(block, land.at[slots[i] * 2 + x], 14 + i, recv, (z_to * 2 + x_to, rad))

    window_copies = [
        panels(block, land.at[(8 - dz) * 2 + x], i, 0, place(dz, dx)) for i, (dz, dx) in enumerate(window)
    ]
    own_copy = pltpu.make_async_copy(block, land.at[16 + x], pan_recv.at[0])
    far_regions = ((1, 3, 6), (2, 11, 14), (3, 0, 3), (4, 14, 16))

    @pl.when(gap)
    def _():
        for i, k in enumerate(slots):
            for recv, low, high in far_regions:

                @pl.when((k >= low) & (k < high))
                def _():
                    direct_copy(i, recv).start()

        for copy in window_copies:
            copy.start()
        own_copy.start()

    def az_copy(src, dst, i, who):
        return pltpu.make_async_remote_copy(
            src_ref=src, dst_ref=dst, send_sem=az_send.at[i], recv_sem=az_recv.at[i],
            device_id=(who, rad), device_id_type=MESH)

    down_copy = az_copy(to_prev, from_next, 0, prev)
    up_copy = az_copy(to_next, from_prev, 1, nxt)
    down_copy.start()
    up_copy.start()

    def rad_copy(src, dst, i, who):
        return pltpu.make_async_remote_copy(
            src_ref=src, dst_ref=dst, send_sem=rad_send.at[i], recv_sem=rad_recv.at[i],
            device_id=(az, who), device_id_type=MESH)

    left_copies = (rad_copy(left_main, in_right_main, 0, rad - 1), rad_copy(left_corner, in_right_corner, 1, rad - 1))
    right_copies = (rad_copy(right_main, in_left_main, 2, rad + 1), rad_copy(right_corner, in_left_corner, 3, rad + 1))

    def send_strips(i):
        @pl.when(has_left)
        def _():
            left_copies[i].start()

        @pl.when(has_right)
        def _():
            right_copies[i].start()

    @pl.when(jnp.logical_not(early))
    def _():
        columns()

    send_strips(0)

    down_copy.wait()
    up_copy.wait()
    for f in range(NF):
        a_ext[f, last : last + 3, :] = from_next[3 * f : 3 * f + 3, :]
        c_ext[f, last : last + 1, :] = from_next[33 + f : 34 + f, :]
        a_ext[f, B - 2 : B, :] = from_prev[2 * f : 2 * f + 2, :]
        c_ext[f, B - 1 : B, :] = from_prev[24 + f : 25 + f, :]
    for l in range(L):
        m_ext[l, last : last + 2, :] = from_next[27 + 2 * l : 29 + 2 * l, :].astype(jnp.int32)
        m_ext[l, B - 2 : B, :] = from_prev[18 + 2 * l : 20 + 2 * l, :].astype(jnp.int32)

    ends = slice(rows, STRIP)
    fields = [(a_ext, s_a, f) for f in range(NF)] + [(c_ext, s_c, f) for f in range(NF)] + [(m_ext, s_m, l) for l in range(L)]
    for low in range(0, len(fields), 8):
        some = fields[low : low + 8]
        stack = []
        for buf, _, f in some:
            stack += [buf[f, B - 8 : B, :].astype(F32), buf[f, last : last + 8, :].astype(F32)]
        if len(some) < 8:
            stack.append(jnp.zeros((LANES - 16 * len(some), LANES), F32))
        turned = jnp.concatenate(stack, axis=0).T
        for place_in, (_, dst, f) in enumerate(some):
            shift = (LANES - 8 - 16 * place_in) % LANES
            dst[f, 2:8, ends] = pltpu.roll(turned[0:8], shift, 1)[0:6]
            dst[f, 8:13, ends] = pltpu.roll(turned[LANES - 8 : LANES], shift, 1)[3:8]

    pack(LANES, ends, left_corner, right_corner)
    send_strips(1)

    def region(low, high, recv):
        view = land.at[pl.ds(low, high - low)]
        return pltpu.make_async_copy(view, view, pan_recv.at[recv])

    two_up = panels(land.at[pl.ds(12, 6)], land.at[pl.ds(6, 6)], 10, 1, place(3, 0))
    two_down = panels(land.at[pl.ds(16, 6)], land.at[pl.ds(22, 6)], 11, 2, place(-3, 0))
    part_up = panels(part_out.at[0], part_in.at[0], 12, 3, place(3, 0))
    part_down = panels(part_out.at[1], part_in.at[1], 13, 4, place(-3, 0))

    def when_start(flag, copy):
        @pl.when(flag)
        def _():
            copy.start()

    @pl.when(gap)
    def _():
        region(12, 22, 0).wait()
        when_start(up_ok, two_up)
        when_start(down_ok, two_down)

    late = jnp.logical_not(early)

    @pl.when(late)
    def _():
        reluct_inner()
        first_inner()

    def deposit(low, high, tile):
        @pl.loop(low // 2, high // 2)
        def _(pair):
            hits, values = [], []
            for slot in (2 * pair, 2 * pair + 1):
                for part in (0, 1):
                    cell = land[slot, 18 + part : 19 + part, :].astype(jnp.int32) - tile * rows
                    cell = jnp.where(cell < 0, cell + cells, cell)
                    ahead = jnp.where(cell < rows + 8, cell, -1)
                    cell = jnp.where(cell >= cells - 8, cell - (cells - 8) + rows + 8, ahead)
                    places = lax.broadcasted_iota(jnp.int32, (rows + 16, half), 0)
                    hits.append(jnp.where(places == cell, 1.0, 0.0).astype(jnp.bfloat16))
                    ninth = land[slot, 16 + part : 17 + part, :]
                    values.append(jnp.concatenate(
                        [land[slot, 8 * part : 8 * part + 8, :], ninth, jnp.zeros((7, half), F32)], axis=0))
            value = jnp.concatenate(values, axis=1)
            first = value.astype(jnp.bfloat16)
            rest = value - first.astype(F32)
            second = rest.astype(jnp.bfloat16)
            third = (rest - second.astype(F32)).astype(jnp.bfloat16)
            acc[...] += lax.dot_general(
                jnp.concatenate([first, second, third], axis=0), jnp.concatenate(hits, axis=1),
                (((1,), (1,)), ((), ())), preferred_element_type=F32)

    def deposited():
        return acc[0:NF, :] + acc[16 : 16 + NF, :] + acc[32 : 32 + NF, :]

    def pass_on(flag, i, low, high, dz, copy):
        @pl.when(flag)
        def _():
            acc[...] = jnp.zeros_like(acc)
            deposit(low, high, (z + dz + n_z) % n_z * 2 + x)
            part_out[i] = deposited()
            copy.start()

    @pl.when(gap)
    def _():
        region(6, 12, 1).wait()
        pass_on(up_ok, 0, 6, 12, 3, part_up)
        region(22, 28, 2).wait()
        pass_on(down_ok, 1, 22, 26, -3, part_down)

    reluct_outer()
    first_outer()

    @pl.when(late)
    def _():
        second_inner()

    second_outer()

    @pl.when(gap)
    def _():
        acc[...] = jnp.zeros_like(acc)
        deposit(6, 28, az)

    @pl.when(has_right)
    def _():
        for i, (came, lanes) in enumerate(((in_right_main, slice(0, rows)), (in_right_corner, ends))):
            rad_copy(left_main if i == 0 else left_corner, came, i, rad + 1).wait_recv()
            for f in range(NF):
                s_a[f, 13:16, lanes] = came[3 * f : 3 * f + 3, :]
                s_c[f, 13:14, lanes] = came[33 + f : 34 + f, :]
            for l in range(L):
                s_m[l, 13:15, lanes] = came[27 + 2 * l : 29 + 2 * l, :]

    @pl.when(has_left)
    def _():
        for i, (came, lanes) in enumerate(((in_left_main, slice(0, rows)), (in_left_corner, ends))):
            rad_copy(right_main if i == 0 else right_corner, came, i + 2, rad - 1).wait_recv()
            for f in range(NF):
                s_a[f, 0:2, lanes] = came[2 * f : 2 * f + 2, :]
                s_c[f, 1:2, lanes] = came[24 + f : 25 + f, :]
            for l in range(L):
                s_m[l, 0:2, lanes] = came[18 + 2 * l : 20 + 2 * l, :]

    @pl.when(jnp.logical_not(has_right))
    def _():
        for f in range(NF):
            s_a[f, 13:16, :] = jnp.zeros((3, STRIP), F32)
        for l in range(L):
            s_m[l, 13:15, :] = jnp.zeros((2, STRIP), F32)

    @pl.when(jnp.logical_not(has_left))
    def _():
        for f in range(NF):
            s_a[f, 0:2, :] = jnp.zeros((2, STRIP), F32)
        for l in range(L):
            s_m[l, 0:2, :] = jnp.zeros((2, STRIP), F32)

    column = lax.broadcasted_iota(jnp.int32, (16, STRIP), 0)
    outside = ((column < 2) & (rad == 0)) | ((column > 12) & (rad == n_rad - 1))
    after = lambda v: pltpu.roll(v, STRIP - 1, 1)
    before = lambda v: pltpu.roll(v, 1, 1)
    right_of = lambda v: pltpu.roll(v, 15, 0)
    left_of = lambda v: pltpu.roll(v, 1, 0)

    for l in range(L):
        flux_sq = jnp.zeros((16, STRIP), F32)
        for c in range(3):
            here = s_a[c * L + l]
            along, across = after(here) - here, right_of(here) - here
            flux_sq = flux_sq + along * along + across * across
        q = half_reluct(s_m[l].astype(jnp.int32), flux_sq, nu_half, sat_of)
        s_q[l] = jnp.where(outside, 0.0, q)

    def strip_faces(l):
        q = s_q[l]
        return faces_of(
            q, after(q), before(q), right_of(q), left_of(q),
            s_q[l + 1] if l + 1 < L else None, s_q[l - 1] if l > 0 else None)

    def strip_neighbours(field, c, l):
        here = field[c * L + l]
        return [
            after(here), before(here), right_of(here), left_of(here),
            field[c * L + l + 1] if l + 1 < L else None, field[c * L + l - 1] if l > 0 else None]

    for l in range(L):
        faces = strip_faces(l)
        inverse = 1.0 / (1.0 + sum(faces[1:], faces[0]))
        s_inv[l] = inverse
        for c in range(3):
            swept = sweep(strip_neighbours(s_a, c, l), s_c[c * L + l], faces, inverse)
            s_v[c * L + l] = jnp.where(outside, 0.0, swept)

    @pl.when(gap)
    def _():
        @pl.when(z < SERVED)
        def _():
            region(0, 6, 3).wait()
            region(28, 32, 4).wait()
            deposit(0, 6, az)
            deposit(28, 32, az)
            spread[0:NF, 0 : rows + 16] = deposited()

        @pl.when(z >= SERVED)
        def _():
            part_up.wait_recv()
            part_down.wait_recv()
            spread[0:NF, 0 : rows + 16] = deposited() + (part_in[0] + part_in[1])

        summed = spread[...]
        lanes_of = lax.broadcasted_iota(jnp.int32, (16, STRIP), 1)
        airgap = jnp.where(lanes_of >= STRIP - 8, pltpu.roll(summed, STRIP - rows - 16, 1), summed)

        @pl.when(rad == stator)
        def _():
            for f in range(NF):
                row = airgap[f : f + 1]
                s_c[f, 2:3, :] = s_c[f, 2:3, :] + row
                s_v[f, 2:3, :] = s_v[f, 2:3, :] + row * s_inv[f % L, 2:3, :]

        @pl.when(rad == stator - 1)
        def _():
            for f in range(NF):
                s_v[f, 13:14, :] = s_v[f, 13:14, :] + airgap[f : f + 1] * s_inv[f % L, 13:14, :]

    lane = lax.broadcasted_iota(jnp.int32, (LANES, LANES), 1)
    edge = (lane < 2) | (lane > LANES - 4)
    for l in range(L):
        faces = strip_faces(l)
        for c in range(3):
            f = c * L + l
            done = sweep(strip_neighbours(s_v, c, l), s_c[f], faces, s_inv[l])
            stacked[8 * f : 8 * f + 3, :] = done[10:13, 0:rows]
            stacked[8 * f + 3 : 8 * f + 5, :] = done[2:4, 0:rows]
    for part in (0, 1):
        here = slice(part * LANES, (part + 1) * LANES)
        turned = stacked[:, here].T
        for f in range(NF):
            out[f, here, :] = jnp.where(edge, pltpu.roll(turned, (LANES - 3 - 8 * f) % LANES, 1), out[f, here, :])

    for i in (0, 1):
        @pl.when(has_left)
        def _():
            left_copies[i].wait_send()

        @pl.when(has_right)
        def _():
            right_copies[i].wait_send()

    @pl.when(gap)
    def _():
        for copy in window_copies:
            copy.wait_send()

        for i in range(len(served)):

            @pl.when(direct[i])
            def _():
                direct_copy(i, 1).wait_send()

        @pl.when(up_ok)
        def _():
            two_up.wait_send()
            part_up.wait_send()

        @pl.when(down_ok)
        def _():
            two_down.wait_send()
            part_down.wait_send()


def local(potential, current, material, nu_table, sat_table, panel_flux, panel_jitter, rotor_offset):
    rows, lanes = potential.shape[2:]
    vmem = lambda *shape: pltpu.VMEM(shape, F32)
    tall = rows + 2 * B
    hbm = pl.BlockSpec(memory_space=pltpu.HBM)
    whole = pl.BlockSpec(memory_space=pltpu.VMEM)
    result = pl.pallas_call(
        kernel,
        out_shape=jax.ShapeDtypeStruct((NF, rows, lanes), F32),
        in_specs=[hbm] * 7 + [pl.BlockSpec(memory_space=pltpu.SMEM)],
        out_specs=whole,
        scratch_shapes=[
            pltpu.SMEM((MAT,), F32), pltpu.SMEM((MAT,), F32), vmem(*panel_flux.shape),
            pltpu.VMEM(panel_jitter.shape, jnp.int32),
            vmem(NF, tall, lanes), vmem(NF, tall, lanes), pltpu.VMEM((L, tall, lanes), jnp.int32),
            vmem(L, tall, lanes), vmem(L, tall, lanes), vmem(NF, tall, lanes),
            vmem(TO_LEFT, lanes), vmem(TO_RIGHT, lanes), vmem(TO_RIGHT, lanes), vmem(TO_LEFT, lanes),
            vmem(TO_LEFT, rows), vmem(TO_LEFT, LANES), vmem(TO_RIGHT, rows), vmem(TO_RIGHT, LANES),
            vmem(TO_LEFT, rows), vmem(TO_LEFT, LANES), vmem(TO_RIGHT, rows), vmem(TO_RIGHT, LANES),
            vmem(NF, 16, STRIP), vmem(L, 16, STRIP), vmem(NF, 16, STRIP),
            vmem(L, 16, STRIP), vmem(L, 16, STRIP), vmem(NF, 16, STRIP),
            vmem(20, LANES), vmem(32, 20, LANES), vmem(48, rows + 16), vmem(16, STRIP), vmem(LANES, rows),
            vmem(2, NF, rows + 16), vmem(2, NF, rows + 16),
            pltpu.SemaphoreType.DMA((7,)), pltpu.SemaphoreType.DMA((2,)), pltpu.SemaphoreType.DMA((2,)),
            pltpu.SemaphoreType.DMA((4,)), pltpu.SemaphoreType.DMA((4,)),
            pltpu.SemaphoreType.DMA((14 + 2 * SERVED,)), pltpu.SemaphoreType.DMA((5,)),
        ],
        compiler_params=pltpu.CompilerParams(
            collective_id=0, has_side_effects=True, vmem_limit_bytes=48 * 1024 * 1024
        ),
    )(
        *[
            pltpu.with_memory_space_constraint(v, pltpu.HBM)
            for v in (
                potential.reshape(NF, rows, lanes), current.reshape(NF, rows, lanes), material,
                nu_table, sat_table, panel_flux, panel_jitter)
        ],
        rotor_offset,
    )
    return result.reshape(potential.shape)


def solution(mesh):
    placed = (
        P(None, None, "az", "rad"),
        P(None, None, "az", "rad"),
        P(None, "az", "rad"),
        P(),
        P(),
        P(None, "az"),
        P("az"),
        P(),
    )
    return jax.shard_map(
        local, mesh=mesh, in_specs=placed, out_specs=P(None, None, "az", "rad"), check_vma=False
    )
```
